256 devices in a mesh: space: 8 (over z), mem: 32 (over x, y, core).
Axes of the slice: x: 4, y: 4, z: 8, core: 2. Of those that a mesh axis runs over, the one named last changes fastest.
Arguments:
- deviations: bfloat16 [1024, 524288], P('mem', 'space'), may hold values from -6 to 6
- obs_cell: int32 [524288], P(('space', 'mem')), may hold values from 0 to 2047, as said below
- obs_weight: float32 [524288], P(('space', 'mem')), may hold values from 0.5 to 6
- block_obs: int32 [4096, 128], P(('space', 'mem')), may hold values from 0 to 524287, as said below
- block_count: int32 [4096], P(('space', 'mem')), may hold values from 32 to 128, as said below
Outputs:
- analysis: bfloat16 [1024, 524288], P('mem', 'space')
The draws below stay inside these ranges and needn't reach their ends.
Inputs may be any that keep to these rules, and one draw needn't show every extreme that they name: `obs_cell`: within each device's 2048 observations the cells do not decrease. `block_obs`: each block's list holds 128 different observation numbers, all held by the block's own device or within 1024 numbers of that device's range. Only the first block_count[b] entries of block b's list are used; some block uses all 128.
All inputs are finite; a program needn't handle non-finite values.
Results may differ from the reference program's by a relative error of at most 0.0026.
Values may be sent and summed in bfloat16 or wider, within the bound.
No kernel may reach another device: no remote copies, remote signals or barrier semaphores. Data moves between devices by JAX's collectives and lax.ppermute only.
A program may use at most 128 MiB of HBM per device.

```python
import math
import jax
import jax.numpy as jnp
from jax import lax

M = 1024
CD = 2048
CB = 128
KOBS = 128
OBS_DEV = 2048
NCELLS = 524288
NOBS = 524288
NBLOCKS = 4096


def draw_obs_cell(key, part):
    devices = NOBS // OBS_DEV
    picked = jax.random.randint(jax.random.fold_in(key, 11), (devices, OBS_DEV), 0, CD)
    return jnp.sort(picked, axis=1).reshape(NOBS).astype(jnp.int32)


def draw_block_obs(key, part):
    blocks_dev = CD // CB
    span = OBS_DEV + OBS_DEV // blocks_dev
    block_ids = jnp.arange(NBLOCKS, dtype=jnp.int32)
    device = block_ids // blocks_dev
    within = block_ids % blocks_dev
    window_start = device * OBS_DEV + within * (OBS_DEV // blocks_dev) - OBS_DEV // 2
    offset = jnp.arange(span, dtype=jnp.int32)
    number = window_start[:, None] + offset[None, :]
    valid = (number >= 0) & (number < NOBS)
    scores = jax.random.randint(jax.random.fold_in(key, 23), (NBLOCKS, span), 0, 1 << 19)
    scores = scores * span + offset[None, :]
    scores = jnp.where(valid, scores, -1)
    _, chosen = lax.top_k(scores, KOBS)
    return jnp.take_along_axis(number, chosen, axis=1).astype(jnp.int32)


def draw_block_count(key, part):
    counts = jax.random.randint(jax.random.fold_in(key, 37), (NBLOCKS,), KOBS // 4, KOBS + 1)
    chosen = jax.random.randint(jax.random.fold_in(key, 41), (), 0, NBLOCKS)
    return jnp.where(jnp.arange(NBLOCKS) == chosen, KOBS, counts).astype(jnp.int32)


def levels(own_key, dims, cuts, least, high):
    def one(axis_at, blocks):
        steps = jax.random.uniform(jax.random.fold_in(jax.random.fold_in(own_key, 6), axis_at), (blocks,), jnp.float32, least / len(cuts), high / len(cuts))
        return jnp.repeat(jnp.exp(steps), dims[axis_at] // blocks).reshape((-1,) + (1,) * (len(dims) - axis_at - 1))

    gain = one(*cuts[0])
    for cut in cuts[1:]:
        gain = gain * one(*cut)
    return gain


def gaussian(rng, extent, spread, bound, split=(), held_as=jnp.bfloat16):
    entries = jax.random.normal(rng, extent, jnp.float32) * spread
    if len(split) > 0:
        entries = levels(rng, extent, split, -0.22, 0.18) * entries
    return jnp.clip(entries, min=-bound, max=bound).astype(held_as)


def setup_inputs(seed: int = 0) -> dict:
    keys = jax.random.split(jax.random.key(seed), 6)
    return {
        "deviations": gaussian(keys[0], (M, NCELLS), 1.0, 6.0, ((0, 32), (1, 8))),
        "obs_cell": draw_obs_cell(jax.random.fold_in(keys[5], 71), 0),
        "obs_weight": jnp.clip(jnp.exp(math.log(6.0) - 2.4849066 * jax.random.uniform(keys[2], (NOBS,), jnp.float32) ** levels(keys[2], (NOBS,), ((0, 256),), -0.2, 0.2)), 0.5, 6.0),
        "block_obs": draw_block_obs(jax.random.fold_in(keys[5], 71), 0),
        "block_count": draw_block_count(jax.random.fold_in(keys[5], 71), 0),
    }


def reference(deviations, obs_cell, obs_weight, block_obs, block_count):
    members = deviations.shape[0]
    weight = obs_weight * (1.0 / math.sqrt(members - 1))
    owner = jnp.arange(NOBS, dtype=jnp.int32) // OBS_DEV
    position = (owner * CD + obs_cell).astype(jnp.int32)
    projected = (jnp.take(deviations, position, axis=1).astype(jnp.float32) * weight[None, :]).astype(jnp.bfloat16)
    slot_ids = jnp.arange(KOBS, dtype=jnp.int32)
    eye_obs = jnp.eye(KOBS, dtype=jnp.float32)

    def update(block_id):
        columns = jnp.take(projected, block_obs[block_id], axis=1)
        columns = jnp.where(slot_ids[None, :] < block_count[block_id], columns, jnp.zeros_like(columns))
        states = lax.dynamic_slice_in_dim(deviations, (block_id * CB).astype(jnp.int32), CB, 1)
        inner = eye_obs + jnp.dot(columns.T.astype(jnp.float32), columns.astype(jnp.float32), preferred_element_type=jnp.float32)
        factor = jnp.linalg.cholesky(inner)
        moved = jnp.dot(columns.T.astype(jnp.float32), states.astype(jnp.float32), preferred_element_type=jnp.float32)
        solved = jax.scipy.linalg.cho_solve((factor, True), moved)
        updated = states.astype(jnp.float32) - 0.5 * jnp.dot(columns.astype(jnp.float32), solved, precision=lax.Precision.HIGHEST)
        return updated.astype(jnp.bfloat16)
    pieces = lax.map(update, jnp.arange(NBLOCKS, dtype=jnp.int32))
    return jnp.transpose(pieces, (1, 0, 2)).reshape(members, NBLOCKS * CB)
```

```python
import math

import jax
import jax.numpy as jnp
from jax import lax
from jax.experimental import pallas as pl
from jax.experimental.pallas import tpu as pltpu
from jax.sharding import PartitionSpec as P

def with_halo(shard, sides, width):
    edges = {}
    for axis, dim in sides:
        size, length = (lax.axis_size(axis), shard.shape[dim])
        up = [(i, (i + 1) % size) for i in range(size - 1)]
        last = lax.slice_in_dim(shard, length - width, length, axis=dim)
        first = lax.slice_in_dim(shard, 0, width, axis=dim)
        edges[dim] = (
            lax.ppermute(last, axis, up),
            lax.ppermute(first, axis, [(b, a) for a, b in up]),
        )
    done = []
    for _, dim in sides:
        low, high = edges[dim]
        around = [(width, width) if d in done else (0, 0) for d in range(shard.ndim)]
        shard = jnp.concatenate([jnp.pad(low, around), shard, jnp.pad(high, around)], axis=dim)
        done.append(dim)
    return shard


NB = 16

def three_way(v):
    hi = v.astype(jnp.bfloat16)
    rest = v - hi.astype(jnp.float32)
    mid = rest.astype(jnp.bfloat16)
    low = (rest - mid.astype(jnp.float32)).astype(jnp.bfloat16)
    return hi, mid, low

def invert_kernel(inner_ref, out_ref, work):
    nblk, n, _ = inner_ref.shape
    lane = lax.broadcasted_iota(jnp.int32, (1, 1, n), 2)
    sub = lax.broadcasted_iota(jnp.int32, (1, NB, 1), 1)
    work[...] = inner_ref[...]

    def step(_, carry):
        panel = work[:, 0:NB, :]
        for k in range(NB):
            row = panel[:, k:k+1, :]
            col = panel[:, :, k:k+1]
            inv = 1.0 / panel[:, k:k+1, k:k+1]
            scaled = jnp.where(lane == k, inv, row * inv)
            panel = jnp.where(sub == k, scaled, jnp.where(lane == k, 0.0, panel) - col * scaled)
        lane2 = lax.broadcasted_iota(jnp.int32, (1, n), 1)
        seg = lane2 // NB
        pick = lax.broadcasted_iota(jnp.int32, (n - NB, n), 1) % NB
        for b in range(nblk):
            rolled = pltpu.roll(panel[b], n - NB, 1)
            rh, rm, rl = three_way(rolled)
            rhs = jnp.concatenate([rh, rm, rh, rl, rm, rh, rl, rm], axis=0)
            rest = work[b, NB:n, :]
            rep = jnp.take_along_axis(rest, pick, axis=1)
            hi = rep.astype(jnp.bfloat16).astype(jnp.float32)
            d1 = rep - hi
            mid = d1.astype(jnp.bfloat16).astype(jnp.float32)
            low = d1 - mid
            lhs = jnp.where((seg == 0) | (seg == 1) | (seg == 3), hi,
                   jnp.where((seg == 2) | (seg == 4) | (seg == 6), mid, low)).astype(jnp.bfloat16)
            kept = pltpu.roll(jnp.where(lane2 < NB, 0.0, rest), n - NB, 1)
            work[b, 0:n - NB, :] = kept - jnp.dot(lhs, rhs, preferred_element_type=jnp.float32)
            work[b, n - NB:n, :] = rolled
        return carry
    lax.fori_loop(0, n // NB, step, 0)
    out_ref[...] = work[...]

def invert(inner):
    return pl.pallas_call(invert_kernel, out_shape=jax.ShapeDtypeStruct(inner.shape, jnp.float32),
        scratch_shapes=[pltpu.VMEM(inner.shape, jnp.float32)],
        name="invert_blocks")(inner)

def on_device(deviations, obs_cell, obs_weight, block_obs, block_count):
    groups = lax.axis_size("mem")
    members = deviations.shape[0] * groups
    dev_cells = deviations.shape[1] // groups
    obs_dev = obs_cell.shape[0]
    weight = obs_weight * (1.0 / math.sqrt(members - 1))
    regrouped = lax.all_to_all(deviations, "mem", split_axis=1, concat_axis=0, tiled=True)
    projected = (
        jnp.take(regrouped, obs_cell, axis=1).astype(jnp.float32) * weight[None, :]
    ).astype(jnp.bfloat16)
    halo_width = obs_dev // 2
    window = with_halo(projected, ((("space", "mem"), 1),), halo_width)
    line_index = lax.axis_index("space") * groups + lax.axis_index("mem")
    window_start = line_index * obs_dev - halo_width
    local_index = block_obs - window_start
    blocks = block_obs.shape[0]
    block_width = dev_cells // blocks
    kslots = block_obs.shape[1]
    slot_ids = jnp.arange(kslots, dtype=jnp.int32)
    columns = jnp.take(window, local_index, axis=1)
    used = slot_ids[None, :] < block_count[:, None]
    columns = jnp.where(used[None, :, :], columns, jnp.zeros_like(columns))
    states = regrouped.reshape(members, blocks, block_width)
    inner = jnp.eye(kslots, dtype=jnp.float32)[None] + jnp.einsum(
        "mbk,mbl->bkl", columns, columns, preferred_element_type=jnp.float32
    )
    inverse = invert(inner)
    moved = jnp.einsum("mbk,mbc->bkc", columns, states, preferred_element_type=jnp.float32)
    solved = jnp.einsum("bkl,blc->bkc", inverse, moved, precision=lax.Precision.HIGHEST)
    high = solved.astype(jnp.bfloat16)
    low = (solved - high.astype(jnp.float32)).astype(jnp.bfloat16)
    change = jnp.einsum(
        "mbk,bkc->mbc", columns, high, preferred_element_type=jnp.float32
    ) + jnp.einsum("mbk,bkc->mbc", columns, low, preferred_element_type=jnp.float32)
    updated = states.astype(jnp.float32) - 0.5 * change
    analysis = updated.reshape(members, dev_cells).astype(jnp.bfloat16)
    return lax.all_to_all(analysis, "mem", split_axis=0, concat_axis=1, tiled=True)


def solution(mesh):
    in_specs = (
        P("mem", "space"),
        P(("space", "mem")),
        P(("space", "mem")),
        P(("space", "mem"), None),
        P(("space", "mem")),
    )
    out_specs = P("mem", "space")
    return jax.shard_map(
        on_device, mesh=mesh, in_specs=in_specs, out_specs=out_specs, check_vma=False
    )
```

```python
import math

import jax
import jax.numpy as jnp
from jax import lax
from jax.experimental import pallas as pl
from jax.experimental.pallas import tpu as pltpu
from jax.sharding import PartitionSpec as P

NB = 16
TILE = 256
ROWS = (16, 16)

NT = (((1,), (1,)), ((), ()))
TN = (((0,), (0,)), ((), ()))


def dot(a, b, dims=(((1,), (0,)), ((), ())), precision=None):
    return lax.dot_general(a, b, dims, precision=precision, preferred_element_type=jnp.float32)


def project_kernel(cell_ref, cells_ref, weight_ref, states_ref, out_ref, acc_ref):
    tile = pl.program_id(0)
    lane = lax.broadcasted_iota(jnp.int32, (TILE, 128), 1)
    first = cell_ref[tile * TILE] // TILE
    last = cell_ref[tile * TILE + TILE - 1] // TILE
    acc_ref[...] = jnp.zeros_like(acc_ref)
    cells = cells_ref[...]

    def add(step, carry):
        start = pl.multiple_of(step * TILE, TILE)
        pick = jnp.concatenate(
            [(cells == lane + (start + at)).astype(jnp.float32) for at in range(0, TILE, 128)], axis=1
        ).astype(jnp.bfloat16)
        acc_ref[...] += dot(pick, states_ref[:, pl.ds(start, TILE)], NT)
        return carry

    lax.fori_loop(first, last + 1, add, 0)
    out_ref[...] = (acc_ref[...] * weight_ref[:, 0:1]).astype(jnp.bfloat16)


def project(obs_cell, cells, weight, states):
    members, width = states.shape
    obs = obs_cell.shape[0]
    return pl.pallas_call(
        project_kernel,
        grid_spec=pltpu.PrefetchScalarGridSpec(
            num_scalar_prefetch=1,
            grid=(obs // TILE,),
            in_specs=[
                pl.BlockSpec((TILE, 128), lambda i, c: (i, 0)),
                pl.BlockSpec((TILE, 128), lambda i, c: (i, 0)),
                pl.BlockSpec((members, width), lambda i, c: (0, 0)),
            ],
            out_specs=pl.BlockSpec((TILE, members), lambda i, c: (i, 0)),
            scratch_shapes=[pltpu.VMEM((TILE, members), jnp.float32)],
        ),
        out_shape=jax.ShapeDtypeStruct((obs, members), jnp.bfloat16),
        cost_estimate=pl.CostEstimate(
            flops=4 * obs * members * TILE, bytes_accessed=8 * obs * members, transcendentals=0
        ),
        name="project",
    )(obs_cell, cells, weight, states)


def gram_kernel(slots_ref, low_ref, own_ref, high_ref, states_ref, *refs):
    if len(refs) == 5:
        gram_in, moved_in, columns_ref, gram_ref, moved_ref = refs
    else:
        columns_ref, gram_ref, moved_ref = refs
    lane = lax.broadcasted_iota(jnp.int32, (128, 128), 1)
    slots = slots_ref[...]

    def pick(start, length):
        return jnp.concatenate(
            [(slots == lane + at).astype(jnp.float32) for at in range(start, start + length, 128)], axis=1
        ).astype(jnp.bfloat16)

    edge, length = low_ref.shape[0], own_ref.shape[0]
    chosen = (
        dot(pick(0, edge), low_ref[...])
        + dot(pick(edge, length), own_ref[...])
        + dot(pick(edge + length, edge), high_ref[...])
    ).astype(jnp.bfloat16)
    columns_ref[0] = chosen
    gram = dot(chosen, chosen, NT)
    moved = dot(chosen, states_ref[...])
    if len(refs) == 5:
        gram = gram + gram_in[0]
        moved = moved + moved_in[0]
    gram_ref[0] = gram
    moved_ref[0] = moved


def gather_gram(slots, low, own, high, states, before):
    members, width = states.shape
    blocks, kslots = slots.shape[0] // 128, 128
    whole = lambda a: pl.BlockSpec(a.shape, lambda i: (0, 0))
    square = pl.BlockSpec((1, kslots, kslots), lambda i: (i, 0, 0))
    squares = jax.ShapeDtypeStruct((blocks, kslots, kslots), jnp.float32)
    return pl.pallas_call(
        gram_kernel,
        grid=(blocks,),
        in_specs=[
            pl.BlockSpec((128, 128), lambda i: (i, 0)),
            whole(low),
            whole(own),
            whole(high),
            pl.BlockSpec((members, kslots), lambda i: (0, i)),
        ]
        + [square] * len(before),
        out_specs=(pl.BlockSpec((1, kslots, members), lambda i: (i, 0, 0)), square, square),
        out_shape=(jax.ShapeDtypeStruct((blocks, kslots, members), jnp.bfloat16), squares, squares),
        cost_estimate=pl.CostEstimate(
            flops=2 * blocks * kslots * members * 4096, bytes_accessed=16 * members * width, transcendentals=0
        ),
        name="gather_gram",
    )(slots, low, own, high, states, *before)


def three_way(v):
    hi = v.astype(jnp.bfloat16)
    rest = v - hi.astype(jnp.float32)
    mid = rest.astype(jnp.bfloat16)
    low = (rest - mid.astype(jnp.float32)).astype(jnp.bfloat16)
    return hi, mid, low


def invert_kernel(gram_ref, out_ref, work):
    nblk, n, _ = gram_ref.shape
    lane = lax.broadcasted_iota(jnp.int32, (1, 1, n), 2)
    sub = lax.broadcasted_iota(jnp.int32, (1, NB, 1), 1)
    lane2 = lax.broadcasted_iota(jnp.int32, (1, n), 1)
    seg = lane2 // NB
    pick = lax.broadcasted_iota(jnp.int32, (n - NB, n), 1) % NB
    rows = lax.broadcasted_iota(jnp.int32, (1, n, n), 1)
    cols = lax.broadcasted_iota(jnp.int32, (1, n, n), 2)
    work[...] = gram_ref[...] + jnp.where(rows == cols, 1.0, 0.0)

    def step(_, carry):
        panel = work[:, 0:NB, :]
        for k in range(NB):
            row = panel[:, k : k + 1, :]
            col = panel[:, :, k : k + 1]
            inv = 1.0 / panel[:, k : k + 1, k : k + 1]
            scaled = jnp.where(lane == k, inv, row * inv)
            panel = jnp.where(sub == k, scaled, jnp.where(lane == k, 0.0, panel) - col * scaled)
        for b in range(nblk):
            rolled = pltpu.roll(panel[b], n - NB, 1)
            rh, rm, rl = three_way(rolled)
            rhs = jnp.concatenate([rh, rm, rh, rl, rm, rh, rl, rm], axis=0)
            rest = work[b, NB:n, :]
            rep = jnp.take_along_axis(rest, pick, axis=1)
            hi = rep.astype(jnp.bfloat16).astype(jnp.float32)
            d1 = rep - hi
            mid = d1.astype(jnp.bfloat16).astype(jnp.float32)
            low = d1 - mid
            lhs = jnp.where(
                (seg == 0) | (seg == 1) | (seg == 3),
                hi,
                jnp.where((seg == 2) | (seg == 4) | (seg == 6), mid, low),
            ).astype(jnp.bfloat16)
            kept = pltpu.roll(jnp.where(lane2 < NB, 0.0, rest), n - NB, 1)
            work[b, 0 : n - NB, :] = kept - dot(lhs, rhs)
            work[b, n - NB : n, :] = rolled
        return carry

    lax.fori_loop(0, n // NB, step, 0)
    out_ref[...] = work[...]


def invert(gram):
    return pl.pallas_call(
        invert_kernel,
        out_shape=jax.ShapeDtypeStruct(gram.shape, jnp.float32),
        scratch_shapes=[pltpu.VMEM(gram.shape, jnp.float32)],
        name="invert_blocks",
    )(gram)


def update_kernel(inverse_ref, moved_ref, *refs):
    out_ref = refs[-1]
    chunks = (len(refs) - 1) // 2
    solved = dot(inverse_ref[0], moved_ref[0], precision=lax.Precision.HIGHEST) * 0.5
    high = solved.astype(jnp.bfloat16)
    low = (solved - high.astype(jnp.float32)).astype(jnp.bfloat16)
    at = 0
    for columns_ref, states_ref in zip(refs[:chunks], refs[chunks:-1]):
        columns = columns_ref[0]
        change = dot(columns, high, TN) + dot(columns, low, TN)
        updated = states_ref[...].astype(jnp.float32) - change
        groups = out_ref.shape[0]
        rows = updated.shape[0] // groups
        out_ref[:, at : at + rows, :] = updated.reshape(groups, rows, 128).astype(jnp.bfloat16)
        at += rows


def update(inverse, moved, columns, states, groups):
    blocks, kslots, _ = inverse.shape
    square = pl.BlockSpec((1, kslots, kslots), lambda i: (i, 0, 0))
    members = sum(s.shape[0] for s in states)
    width = states[0].shape[1]
    return pl.pallas_call(
        update_kernel,
        grid=(blocks,),
        in_specs=[square, square]
        + [pl.BlockSpec((1, kslots, c.shape[2]), lambda i: (i, 0, 0)) for c in columns]
        + [pl.BlockSpec((s.shape[0], kslots), lambda i: (0, i)) for s in states],
        out_specs=pl.BlockSpec((groups, members // groups, kslots), lambda i: (0, 0, i)),
        out_shape=jax.ShapeDtypeStruct((groups, members // groups, width), jnp.bfloat16),
        name="update",
    )(inverse, moved, *columns, *states)


def on_device(deviations, obs_cell, obs_weight, block_obs, block_count):
    groups = lax.axis_size("mem")
    members = deviations.shape[0] * groups
    obs_dev = obs_cell.shape[0]
    edge = obs_dev // 2
    weight = obs_weight * (1.0 / math.sqrt(members - 1))
    cells = jnp.broadcast_to(obs_cell[:, None], (obs_dev, 128))
    weights = jnp.broadcast_to(weight[:, None], (obs_dev, 128))
    line_index = lax.axis_index("space") * groups + lax.axis_index("mem")
    local_index = block_obs - (line_index * obs_dev - edge)
    slot_ids = jnp.arange(block_obs.shape[1], dtype=jnp.int32)
    local_index = jnp.where(slot_ids[None, :] < block_count[:, None], local_index, -1)
    slots = jnp.broadcast_to(local_index.reshape(-1)[:, None], (local_index.size, 128))
    size = lax.axis_size("space") * groups
    up = [(i, i + 1) for i in range(size - 1)]
    down = [(b, a) for a, b in up]
    at = 0
    states, columns, before = [], [], ()
    for rows in ROWS:
        part = lax.slice_in_dim(deviations, at, at + rows, axis=0)
        at += rows
        moved_in = lax.all_to_all(part, "mem", split_axis=1, concat_axis=0, tiled=True)
        own = project(obs_cell, cells, weights, moved_in)
        low = lax.ppermute(own[edge:], ("space", "mem"), up)
        high = lax.ppermute(own[:edge], ("space", "mem"), down)
        chosen, *before = gather_gram(slots, low, own, high, moved_in, before)
        states.append(moved_in)
        columns.append(chosen)
    gram, moved = before
    analysis = update(invert(gram), moved, columns, states, groups)
    return lax.all_to_all(
        analysis.reshape(members, -1), "mem", split_axis=0, concat_axis=1, tiled=True
    )


def solution(mesh):
    in_specs = (
        P("mem", "space"),
        P(("space", "mem")),
        P(("space", "mem")),
        P(("space", "mem"), None),
        P(("space", "mem")),
    )
    out_specs = P("mem", "space")
    return jax.shard_map(
        on_device, mesh=mesh, in_specs=in_specs, out_specs=out_specs, check_vma=False
    )
```

```python
import math

import jax
import jax.numpy as jnp
from jax import lax
from jax.experimental import pallas as pl
from jax.experimental.pallas import tpu as pltpu
from jax.sharding import PartitionSpec as P

NB = 16
TILE = 256
CHUNKS = 2
SPAN = 512
SPREAD = 32

NT = (((1,), (1,)), ((), ()))
TN = (((0,), (0,)), ((), ()))


def dot(a, b, dims=(((1,), (0,)), ((), ())), precision=None):
    return lax.dot_general(a, b, dims, precision=precision, preferred_element_type=jnp.float32)


def stage_kernel(in_ref, out_ref):
    width = out_ref.shape[2]
    for at in range(out_ref.shape[0]):
        out_ref[at] = in_ref[:, at * width : (at + 1) * width]


def stage(deviations, chunk, rows, groups, per_step=8):
    width = deviations.shape[1] // groups
    return pl.pallas_call(
        stage_kernel,
        grid=(groups // per_step,),
        in_specs=[pl.BlockSpec((rows, width * per_step), lambda i: (chunk, i))],
        out_specs=pl.BlockSpec((per_step, rows, width), lambda i: (i, 0, 0)),
        out_shape=jax.ShapeDtypeStruct((groups, rows, width), deviations.dtype),
        cost_estimate=pl.CostEstimate(
            flops=0, bytes_accessed=4 * groups * rows * width, transcendentals=0
        ),
        name="stage",
    )(deviations)


def project_kernel(cell_ref, cells_ref, weight_ref, states_ref, first_ref, last_ref, acc_ref):
    tile = pl.program_id(0)
    half = pl.num_programs(0) // 2
    width = states_ref.shape[1]
    lane = lax.broadcasted_iota(jnp.int32, (TILE, 128), 1)
    begin = jnp.minimum(cell_ref[tile * TILE] // 128 * 128, width - SPAN)
    end = cell_ref[tile * TILE + TILE - 1]
    cells = cells_ref[...]

    def picked(cells, start):
        start = pl.multiple_of(start, 128)
        pick = jnp.concatenate(
            [(cells == lane + (start + at)).astype(jnp.float32) for at in range(0, SPAN, 128)], axis=1
        ).astype(jnp.bfloat16)
        return dot(pick, states_ref[:, pl.ds(start, SPAN)], NT)

    acc_ref[...] = picked(cells, begin)

    def add(step, carry):
        lower = begin + step * SPAN
        acc_ref[...] += picked(
            jnp.where(cells >= lower, cells, -1), jnp.minimum(lower, width - SPAN)
        )
        return carry

    lax.fori_loop(1, (end - begin) // SPAN + 1, add, 0)
    done = (acc_ref[...] * weight_ref[:, 0:1]).astype(jnp.bfloat16)

    @pl.when(tile < half)
    def _():
        first_ref[...] = done

    @pl.when(tile >= half)
    def _():
        last_ref[...] = done


def project(obs_cell, cells, weight, states):
    members, width = states.shape
    obs = obs_cell.shape[0]
    half = obs // TILE // 2
    side = jax.ShapeDtypeStruct((obs // 2, members), jnp.bfloat16)
    return pl.pallas_call(
        project_kernel,
        grid_spec=pltpu.PrefetchScalarGridSpec(
            num_scalar_prefetch=1,
            grid=(obs // TILE,),
            in_specs=[
                pl.BlockSpec((TILE, 128), lambda i, c: (i, 0)),
                pl.BlockSpec((TILE, 128), lambda i, c: (i, 0)),
                pl.BlockSpec((members, width), lambda i, c: (0, 0)),
            ],
            out_specs=(
                pl.BlockSpec((TILE, members), lambda i, c: (jnp.minimum(i, half - 1), 0)),
                pl.BlockSpec((TILE, members), lambda i, c: (jnp.maximum(i - half, 0), 0)),
            ),
            scratch_shapes=[pltpu.VMEM((TILE, members), jnp.float32)],
        ),
        out_shape=(side, side),
        cost_estimate=pl.CostEstimate(
            flops=2 * obs * members * SPAN, bytes_accessed=8 * obs * members, transcendentals=0
        ),
        name="project",
    )(obs_cell, cells, weight, states)


def gram_kernel(slot_ref, *refs):
    pieces, states = refs[: 4 * CHUNKS], refs[4 * CHUNKS : 5 * CHUNKS]
    columns_ref, gram_ref, moved_ref, rows_ref, picked_ref = refs[5 * CHUNKS :]
    block = pl.program_id(0)
    edge, part = pieces[0].shape
    tiles = part // 128
    width = CHUNKS * tiles
    kslots = gram_ref.shape[1]

    def gather(block, slot):
        for k in range(kslots):
            row = pl.multiple_of(slot_ref[block * kslots + k] * width, width)
            picked_ref[slot, k * width : (k + 1) * width, :] = rows_ref[pl.ds(row, width), :]

    @pl.when(block == 0)
    def _():
        for side in range(4):
            for chunk in range(CHUNKS):
                source = pieces[chunk * 4 + side]

                def spread(step, carry):
                    start = pl.multiple_of(step * SPREAD, SPREAD)
                    for tile in range(tiles):
                        value = source[pl.ds(start, SPREAD), tile * 128 : (tile + 1) * 128]
                        row = (side * edge + start) * width + chunk * tiles + tile
                        rows_ref[pl.ds(row, SPREAD, stride=width), :] = value.astype(jnp.float32)
                    return carry

                lax.fori_loop(0, edge // SPREAD, spread, 0)
        rows_ref[4 * edge * width :, :] = jnp.zeros((width, 128), jnp.float32)
        gather(0, 0)

    now = lax.rem(block, 2)
    gather(jnp.minimum(block + 1, pl.num_programs(0) - 1), 1 - now)
    chosen = jnp.concatenate(
        [picked_ref[now, pl.ds(at, kslots, stride=width), :].astype(jnp.bfloat16) for at in range(width)],
        axis=1,
    )
    columns_ref[0] = chosen
    gram_ref[0] = dot(chosen, chosen, NT)
    moved = 0.0
    for chunk in range(CHUNKS):
        moved = moved + dot(chosen[:, chunk * part : (chunk + 1) * part], states[chunk][...])
    moved_ref[0] = moved


def gather_gram(slots, pieces, states, blocks):
    part, width = states[0].shape
    members = part * CHUNKS
    edge = pieces[0].shape[0]
    kslots = slots.shape[0] // blocks
    square = pl.BlockSpec((1, kslots, kslots), lambda i, s: (i, 0, 0))
    squares = jax.ShapeDtypeStruct((blocks, kslots, kslots), jnp.float32)
    lanes = members // 128
    return pl.pallas_call(
        gram_kernel,
        grid_spec=pltpu.PrefetchScalarGridSpec(
            num_scalar_prefetch=1,
            grid=(blocks,),
            in_specs=[pl.BlockSpec((edge, part), lambda i, s: (0, 0), pipeline_mode=pl.Buffered(1))] * len(pieces)
            + [pl.BlockSpec((part, width // blocks), lambda i, s: (0, i))] * CHUNKS,
            out_specs=(
                pl.BlockSpec((1, kslots, members), lambda i, s: (i, 0, 0)),
                square,
                square,
            ),
            scratch_shapes=[
                pltpu.VMEM(((4 * edge + 1) * lanes, 128), jnp.float32),
                pltpu.VMEM((2, kslots * lanes, 128), jnp.float32),
            ],
        ),
        out_shape=(jax.ShapeDtypeStruct((blocks, kslots, members), jnp.bfloat16), squares, squares),
        compiler_params=pltpu.CompilerParams(vmem_limit_bytes=48 * 1024 * 1024),
        cost_estimate=pl.CostEstimate(
            flops=4 * blocks * kslots * kslots * members,
            bytes_accessed=16 * members * width,
            transcendentals=0,
        ),
        name="gather_gram",
    )(slots, *pieces, *states)


def three_way(v):
    hi = v.astype(jnp.bfloat16)
    rest = v - hi.astype(jnp.float32)
    mid = rest.astype(jnp.bfloat16)
    low = (rest - mid.astype(jnp.float32)).astype(jnp.bfloat16)
    return hi, mid, low


def invert_kernel(gram_ref, out_ref, work):
    nblk, n, _ = gram_ref.shape
    lane = lax.broadcasted_iota(jnp.int32, (1, 1, n), 2)
    sub = lax.broadcasted_iota(jnp.int32, (1, NB, 1), 1)
    lane2 = lax.broadcasted_iota(jnp.int32, (1, n), 1)
    rows = lax.broadcasted_iota(jnp.int32, (1, n, n), 1)
    cols = lax.broadcasted_iota(jnp.int32, (1, n, n), 2)
    work[...] = gram_ref[...] + jnp.where(rows == cols, 1.0, 0.0)

    def step(number, carry):
        panel = work[:, 0:NB, :]
        flip = lane2 >= n - number * NB
        sides = jnp.where(flip[None], -panel, panel)
        for k in range(NB):
            row = panel[:, k : k + 1, :]
            col = panel[:, :, k : k + 1]
            inv = 1.0 / panel[:, k : k + 1, k : k + 1]
            scaled = jnp.where(lane == k, inv, row * inv)
            panel = jnp.where(sub == k, scaled, jnp.where(lane == k, 0.0, panel) - col * scaled)
        for b in range(nblk):
            rolled = pltpu.roll(panel[b], n - NB, 1)
            rh, rm, rl = three_way(rolled)
            ch, cm, cl = three_way(sides[b])
            rhs = jnp.concatenate([rh, rm, rh, rl, rm, rh, rl, rm], axis=0)
            lhs = jnp.concatenate([ch, ch, cm, ch, cm, cl, cm, cl], axis=0)
            change = dot(lhs, rhs, TN)
            kept = pltpu.roll(jnp.where(lane2 < NB, 0.0, work[b, NB:n, :]), n - NB, 1)
            work[b, 0 : n - NB, :] = kept - change[NB:n]
            work[b, n - NB : n, :] = rolled
        return carry

    lax.fori_loop(0, n // NB, step, 0)
    out_ref[...] = work[...]


def invert(gram):
    return pl.pallas_call(
        invert_kernel,
        out_shape=jax.ShapeDtypeStruct(gram.shape, jnp.float32),
        scratch_shapes=[pltpu.VMEM(gram.shape, jnp.float32)],
        name="invert_blocks",
    )(gram)


def update_kernel(inverse_ref, moved_ref, columns_ref, *refs):
    states, out_ref = refs[:-1], refs[-1]
    groups = out_ref.shape[0]
    part = states[0].shape[0]
    rows = part // groups
    for at in range(inverse_ref.shape[0]):
        wh, wm, wl = three_way(inverse_ref[at])
        mh, mm, ml = three_way(moved_ref[at] * 0.5)
        solved = dot(
            jnp.concatenate([wh, wh, wm, wh, wl, wm], axis=1),
            jnp.concatenate([mh, mm, mh, ml, mh, mm], axis=0),
        )
        high = solved.astype(jnp.bfloat16)
        low = (solved - high.astype(jnp.float32)).astype(jnp.bfloat16)
        both = jnp.concatenate([high, low], axis=0)
        columns = columns_ref[at].T
        twice = jnp.concatenate([columns, columns], axis=1)
        cells = slice(at * 128, at * 128 + 128)
        for chunk, states_ref in enumerate(states):
            change = dot(twice[chunk * part : (chunk + 1) * part], both)
            updated = (states_ref[:, cells].astype(jnp.float32) - change).astype(jnp.bfloat16)
            out_ref[:, chunk * rows : (chunk + 1) * rows, cells] = updated.reshape(groups, rows, 128)


def update(inverse, moved, columns, states, groups, per_step=2):
    blocks, kslots, _ = inverse.shape
    square = pl.BlockSpec((per_step, kslots, kslots), lambda i: (i, 0, 0))
    members = columns.shape[2]
    part, width = states[0].shape
    return pl.pallas_call(
        update_kernel,
        grid=(blocks // per_step,),
        in_specs=[square, square, pl.BlockSpec((per_step, kslots, members), lambda i: (i, 0, 0))]
        + [pl.BlockSpec((part, per_step * kslots), lambda i: (0, i))] * len(states),
        out_specs=pl.BlockSpec((groups, members // groups, per_step * kslots), lambda i: (0, 0, i)),
        out_shape=jax.ShapeDtypeStruct((groups, members // groups, width), jnp.bfloat16),
        name="update",
    )(inverse, moved, columns, *states)


def on_device(deviations, obs_cell, obs_weight, block_obs, block_count):
    groups = lax.axis_size("mem")
    members = deviations.shape[0] * groups
    obs_dev = obs_cell.shape[0]
    weight = obs_weight * (1.0 / math.sqrt(members - 1))
    cells = jnp.broadcast_to(obs_cell[:, None], (obs_dev, 128))
    weights = jnp.broadcast_to(weight[:, None], (obs_dev, 128))
    line_index = lax.axis_index("space") * groups + lax.axis_index("mem")
    local_index = block_obs - (line_index * obs_dev - obs_dev // 2)
    slot_ids = jnp.arange(block_obs.shape[1], dtype=jnp.int32)
    slots = jnp.where(slot_ids[None, :] < block_count[:, None], local_index, 2 * obs_dev).reshape(-1)
    size = lax.axis_size("space") * groups
    up = [(i, i + 1) for i in range(size - 1)]
    down = [(b, a) for a, b in up]
    rows = deviations.shape[0] // CHUNKS
    states, pieces = [], []
    for chunk in range(CHUNKS):
        part = stage(deviations, chunk, rows, groups)
        part = lax.all_to_all(part, "mem", split_axis=0, concat_axis=0, tiled=True)
        states.append(part.reshape(groups * rows, -1))
        first, last = project(obs_cell, cells, weights, states[-1])
        low = lax.ppermute(last, ("space", "mem"), up)
        high = lax.ppermute(first, ("space", "mem"), down)
        pieces += [low, first, last, high]
    columns, gram, moved = gather_gram(slots, pieces, states, block_obs.shape[0])
    analysis = update(invert(gram), moved, columns, states, groups)
    return lax.all_to_all(
        analysis.reshape(members, -1), "mem", split_axis=0, concat_axis=1, tiled=True
    )


def solution(mesh):
    in_specs = (
        P("mem", "space"),
        P(("space", "mem")),
        P(("space", "mem")),
        P(("space", "mem"), None),
        P(("space", "mem")),
    )
    out_specs = P("mem", "space")
    return jax.shard_map(
        on_device, mesh=mesh, in_specs=in_specs, out_specs=out_specs, check_vma=False
    )
```

```python
import math

import jax
import jax.numpy as jnp
from jax import lax
from jax.experimental import pallas as pl
from jax.experimental.pallas import tpu as pltpu
from jax.sharding import PartitionSpec as P


NB = 16
TILE = 512
CHUNKS = 2
SPAN = 640
GRAM_STEP = 4
SPREAD = 64

NT = (((1,), (1,)), ((), ()))
TN = (((0,), (0,)), ((), ()))


def dot(a, b, dims=(((1,), (0,)), ((), ())), precision=None):
    return lax.dot_general(a, b, dims, precision=precision, preferred_element_type=jnp.float32)


def stage_kernel(in_ref, out_ref):
    width = out_ref.shape[2]
    for at in range(out_ref.shape[0]):
        out_ref[at] = in_ref[:, at * width : (at + 1) * width]


def stage(deviations, chunk, rows, groups, per_step=8):
    width = deviations.shape[1] // groups
    return pl.pallas_call(
        stage_kernel,
        grid=(groups // per_step,),
        in_specs=[pl.BlockSpec((rows, width * per_step), lambda i: (chunk, i))],
        out_specs=pl.BlockSpec((per_step, rows, width), lambda i: (i, 0, 0)),
        out_shape=jax.ShapeDtypeStruct((groups, rows, width), deviations.dtype),
        cost_estimate=pl.CostEstimate(
            flops=0, bytes_accessed=4 * groups * rows * width, transcendentals=0
        ),
        name="stage",
    )(deviations)


def project_kernel(cell_ref, cells_ref, weight_ref, states_ref, first_ref, last_ref, acc_ref):
    tile = pl.program_id(0)
    half = pl.num_programs(0) // 2
    width = states_ref.shape[1]
    lane = lax.broadcasted_iota(jnp.int32, (TILE, 128), 1)
    begin = jnp.minimum(cell_ref[tile * TILE] // 128 * 128, width - SPAN)
    end = cell_ref[tile * TILE + TILE - 1]
    cells = cells_ref[...]

    def picked(cells, start):
        start = pl.multiple_of(start, 128)
        pick = jnp.concatenate(
            [(cells == lane + (start + at)).astype(jnp.float32) for at in range(0, SPAN, 128)], axis=1
        ).astype(jnp.bfloat16)
        return dot(pick, states_ref[:, pl.ds(start, SPAN)], NT)

    acc_ref[...] = picked(cells, begin)

    def add(step, carry):
        lower = begin + step * SPAN
        acc_ref[...] += picked(
            jnp.where(cells >= lower, cells, -1), jnp.minimum(lower, width - SPAN)
        )
        return carry

    lax.fori_loop(1, (end - begin) // SPAN + 1, add, 0)
    done = (acc_ref[...] * weight_ref[:, 0:1]).astype(jnp.bfloat16)

    @pl.when(tile < half)
    def _():
        first_ref[...] = done

    @pl.when(tile >= half)
    def _():
        last_ref[...] = done


def project(obs_cell, cells, weight, states):
    members, width = states.shape
    obs = obs_cell.shape[0]
    half = obs // TILE // 2
    side = jax.ShapeDtypeStruct((obs // 2, members), jnp.bfloat16)
    return pl.pallas_call(
        project_kernel,
        grid_spec=pltpu.PrefetchScalarGridSpec(
            num_scalar_prefetch=1,
            grid=(obs // TILE,),
            in_specs=[
                pl.BlockSpec((TILE, 128), lambda i, c: (i, 0)),
                pl.BlockSpec((TILE, 128), lambda i, c: (i, 0)),
                pl.BlockSpec((members, width), lambda i, c: (0, 0)),
            ],
            out_specs=(
                pl.BlockSpec((TILE, members), lambda i, c: (jnp.minimum(i, half - 1), 0)),
                pl.BlockSpec((TILE, members), lambda i, c: (jnp.maximum(i - half, 0), 0)),
            ),
            scratch_shapes=[pltpu.VMEM((TILE, members), jnp.float32)],
        ),
        out_shape=(side, side),
        cost_estimate=pl.CostEstimate(
            flops=2 * obs * members * SPAN, bytes_accessed=8 * obs * members, transcendentals=0
        ),
        name="project",
    )(obs_cell, cells, weight, states)


def gram_kernel(slot_ref, *refs):
    pieces, states = refs[: 4 * CHUNKS], refs[4 * CHUNKS : 5 * CHUNKS]
    columns_ref, gram_ref, moved_ref, landed_ref, rows_ref, picked_ref, sems = refs[5 * CHUNKS :]
    step = pl.program_id(0)
    edge, part = pieces[0].shape
    tiles = part // 128
    width = CHUNKS * tiles
    per_step, kslots, _ = gram_ref.shape

    @pl.when(step == 0)
    def _():
        copies = [
            pltpu.make_async_copy(piece, landed_ref.at[at], sems.at[at]) for at, piece in enumerate(pieces)
        ]
        order = [chunk * 4 + side for side in (1, 2, 0, 3) for chunk in range(CHUNKS)]
        for at in order:
            copies[at].start()
        rows_ref[4 * edge * width :, :] = jnp.zeros((width, 128), jnp.float32)
        for at in order:
            chunk, side = divmod(at, 4)
            copies[at].wait()

            def spread(turn, carry):
                start = pl.multiple_of(turn * SPREAD, SPREAD)
                for tile in range(tiles):
                    value = landed_ref[at, pl.ds(start, SPREAD), tile * 128 : (tile + 1) * 128]
                    row = (side * edge + start) * width + chunk * tiles + tile
                    rows_ref[pl.ds(row, SPREAD, stride=width), :] = value.astype(jnp.float32)
                return carry

            lax.fori_loop(0, edge // SPREAD, spread, 0)

    for j in range(per_step):
        for k in range(kslots):
            row = pl.multiple_of(slot_ref[(step * per_step + j) * kslots + k], width)
            picked_ref[j, k * width : (k + 1) * width, :] = rows_ref[pl.ds(row, width), :]
    for j in range(per_step):
        chosen = jnp.concatenate(
            [picked_ref[j, pl.ds(at, kslots, stride=width), :].astype(jnp.bfloat16) for at in range(width)],
            axis=1,
        )
        columns_ref[j] = chosen
        gram_ref[j] = dot(chosen, chosen, NT)
        cells = slice(j * 128, j * 128 + 128)
        moved_ref[j] = dot(chosen, jnp.concatenate([s[:, cells] for s in states], axis=0))


def gather_gram(slots, pieces, states, blocks, per_step=GRAM_STEP):
    part, width = states[0].shape
    members = part * CHUNKS
    edge = pieces[0].shape[0]
    kslots = slots.shape[0] // blocks
    square = pl.BlockSpec((per_step, kslots, kslots), lambda i, s: (i, 0, 0))
    squares = jax.ShapeDtypeStruct((blocks, kslots, kslots), jnp.float32)
    lanes = members // 128
    return pl.pallas_call(
        gram_kernel,
        grid_spec=pltpu.PrefetchScalarGridSpec(
            num_scalar_prefetch=1,
            grid=(blocks // per_step,),
            in_specs=[pl.BlockSpec(memory_space=pl.ANY)] * len(pieces)
            + [pl.BlockSpec((part, per_step * width // blocks), lambda i, s: (0, i))] * CHUNKS,
            out_specs=(
                pl.BlockSpec((per_step, kslots, members), lambda i, s: (i, 0, 0)),
                square,
                square,
            ),
            scratch_shapes=[
                pltpu.VMEM((len(pieces), edge, part), jnp.bfloat16),
                pltpu.VMEM(((4 * edge + 1) * lanes, 128), jnp.float32),
                pltpu.VMEM((per_step, kslots * lanes, 128), jnp.float32),
                pltpu.SemaphoreType.DMA((len(pieces),)),
            ],
        ),
        out_shape=(jax.ShapeDtypeStruct((blocks, kslots, members), jnp.bfloat16), squares, squares),
        compiler_params=pltpu.CompilerParams(vmem_limit_bytes=60 * 1024 * 1024),
        cost_estimate=pl.CostEstimate(
            flops=4 * blocks * kslots * kslots * members,
            bytes_accessed=16 * members * width,
            transcendentals=0,
        ),
        name="gather_gram",
    )(slots, *pieces, *states)


def three_way(v):
    hi = v.astype(jnp.bfloat16)
    rest = v - hi.astype(jnp.float32)
    mid = rest.astype(jnp.bfloat16)
    low = (rest - mid.astype(jnp.float32)).astype(jnp.bfloat16)
    return hi, mid, low


def invert_kernel(gram_ref, out_ref, work):
    nblk, n, _ = gram_ref.shape
    lane = lax.broadcasted_iota(jnp.int32, (8, n), 1)
    sub = lax.broadcasted_iota(jnp.int32, (8, n), 0)
    lane2 = lax.broadcasted_iota(jnp.int32, (1, n), 1)
    rows = lax.broadcasted_iota(jnp.int32, (1, n, n), 1)
    cols = lax.broadcasted_iota(jnp.int32, (1, n, n), 2)
    work[...] = gram_ref[...] + jnp.where(rows == cols, 1.0, 0.0)

    def step(number, carry):
        flip = lane2 >= n - number * NB
        panel = [[work[b, at : at + 8, :] for at in range(0, NB, 8)] for b in range(nblk)]
        for k in range(NB):
            here = lane == k
            own, at = divmod(k, 8)
            for b in range(nblk):
                col = [jnp.broadcast_to(p[:, k : k + 1], (8, n)) for p in panel[b]]
                inv = 1.0 / col[own][at : at + 1, :]
                scaled = jnp.where(here[0:1], inv, panel[b][own][at : at + 1, :] * inv)
                scaled = jnp.broadcast_to(scaled, (8, n))
                new = [jnp.where(here, 0.0, p) - c * scaled for p, c in zip(panel[b], col)]
                new[own] = jnp.where(sub == at, scaled, new[own])
                panel[b] = new
        for b in range(nblk):
            sides = work[b, 0:NB, :]
            sides = jnp.where(flip, -sides, sides)
            rolled = pltpu.roll(jnp.concatenate(panel[b], axis=0), n - NB, 1)
            rh, rm, rl = three_way(rolled)
            ch, cm, cl = three_way(sides)
            rhs = jnp.concatenate([rh, rm, rh, rl, rm, rh, rl, rm], axis=0)
            lhs = jnp.concatenate([ch, ch, cm, ch, cm, cl, cm, cl], axis=0)
            change = dot(lhs, rhs, TN)
            kept = pltpu.roll(jnp.where(lane2 < NB, 0.0, work[b, NB:n, :]), n - NB, 1)
            work[b, 0 : n - NB, :] = kept - change[NB:n]
            work[b, n - NB : n, :] = rolled
        return carry

    lax.fori_loop(0, n // NB, step, 0)
    out_ref[...] = work[...]


def invert(gram):
    return pl.pallas_call(
        invert_kernel,
        out_shape=jax.ShapeDtypeStruct(gram.shape, jnp.float32),
        scratch_shapes=[pltpu.VMEM(gram.shape, jnp.float32)],
        name="invert_blocks",
    )(gram)


def update_kernel(inverse_ref, moved_ref, columns_ref, *refs):
    states, out_ref = refs[:-1], refs[-1]
    groups = out_ref.shape[0]
    part = states[0].shape[0]
    rows = part // groups
    for at in range(inverse_ref.shape[0]):
        wh, wm, wl = three_way(inverse_ref[at])
        mh, mm, ml = three_way(moved_ref[at] * 0.5)
        solved = dot(
            jnp.concatenate([wh, wh, wm, wh, wl, wm], axis=1),
            jnp.concatenate([mh, mm, mh, ml, mh, mm], axis=0),
        )
        high = solved.astype(jnp.bfloat16)
        low = (solved - high.astype(jnp.float32)).astype(jnp.bfloat16)
        both = jnp.concatenate([high, low], axis=0)
        columns = columns_ref[at].T
        twice = jnp.concatenate([columns, columns], axis=1)
        cells = slice(at * 128, at * 128 + 128)
        for chunk, states_ref in enumerate(states):
            change = dot(twice[chunk * part : (chunk + 1) * part], both)
            updated = (states_ref[:, cells].astype(jnp.float32) - change).astype(jnp.bfloat16)
            out_ref[:, chunk * rows : (chunk + 1) * rows, cells] = updated.reshape(groups, rows, 128)


def update(inverse, moved, columns, states, groups, per_step=4):
    blocks, kslots, _ = inverse.shape
    square = pl.BlockSpec((per_step, kslots, kslots), lambda i: (i, 0, 0))
    members = columns.shape[2]
    part, width = states[0].shape
    return pl.pallas_call(
        update_kernel,
        grid=(blocks // per_step,),
        in_specs=[square, square, pl.BlockSpec((per_step, kslots, members), lambda i: (i, 0, 0))]
        + [pl.BlockSpec((part, per_step * kslots), lambda i: (0, i))] * len(states),
        out_specs=pl.BlockSpec((groups, members // groups, per_step * kslots), lambda i: (0, 0, i)),
        out_shape=jax.ShapeDtypeStruct((groups, members // groups, width), jnp.bfloat16),
        name="update",
    )(inverse, moved, columns, *states)


def on_device(deviations, obs_cell, obs_weight, block_obs, block_count):
    groups = lax.axis_size("mem")
    members = deviations.shape[0] * groups
    obs_dev = obs_cell.shape[0]
    weight = obs_weight * (1.0 / math.sqrt(members - 1))
    cells = jnp.broadcast_to(obs_cell[:, None], (obs_dev, 128))
    weights = jnp.broadcast_to(weight[:, None], (obs_dev, 128))
    line_index = lax.axis_index("space") * groups + lax.axis_index("mem")
    local_index = block_obs - (line_index * obs_dev - obs_dev // 2)
    slot_ids = jnp.arange(block_obs.shape[1], dtype=jnp.int32)
    slots = jnp.where(slot_ids[None, :] < block_count[:, None], local_index, 2 * obs_dev)
    slots = slots.reshape(-1) * (members // 128)
    size = lax.axis_size("space") * groups
    up = [(i, i + 1) for i in range(size - 1)]
    down = [(b, a) for a, b in up]
    rows = deviations.shape[0] // CHUNKS
    states, pieces = [], []
    for chunk in range(CHUNKS):
        part = stage(deviations, chunk, rows, groups)
        part = lax.all_to_all(part, "mem", split_axis=0, concat_axis=0, tiled=True)
        states.append(part.reshape(groups * rows, -1))
        first, last = project(obs_cell, cells, weights, states[-1])
        low = lax.ppermute(last, ("space", "mem"), up)
        high = lax.ppermute(first, ("space", "mem"), down)
        pieces += [low, first, last, high]
    columns, gram, moved = gather_gram(slots, pieces, states, block_obs.shape[0])
    analysis = update(invert(gram), moved, columns, states, groups)
    return lax.all_to_all(
        analysis.reshape(members, -1), "mem", split_axis=0, concat_axis=1, tiled=True
    )


def solution(mesh):
    in_specs = (
        P("mem", "space"),
        P(("space", "mem")),
        P(("space", "mem")),
        P(("space", "mem"), None),
        P(("space", "mem")),
    )
    out_specs = P("mem", "space")

    return jax.shard_map(
        on_device, mesh=mesh, in_specs=in_specs, out_specs=out_specs, check_vma=False
    )
```

```python
import math

import jax
import jax.numpy as jnp
from jax import lax
from jax.experimental import pallas as pl
from jax.experimental.pallas import tpu as pltpu
from jax.sharding import PartitionSpec as P


NB = 16
TILE = 512
PIECES = 2
SPAN = 640
GRAM_STEP = 4
SPREAD = 64

NT = (((1,), (1,)), ((), ()))
TN = (((0,), (0,)), ((), ()))


def dot(a, b, dims=(((1,), (0,)), ((), ())), precision=None):
    return lax.dot_general(a, b, dims, precision=precision, preferred_element_type=jnp.float32)


def project_kernel(cell_ref, cells_ref, weight_ref, states_ref, first_ref, last_ref, acc_ref):
    tile = pl.program_id(0)
    half = pl.num_programs(0) // 2
    width = states_ref.shape[1]
    lane = lax.broadcasted_iota(jnp.int32, (TILE, 128), 1)
    begin = jnp.minimum(cell_ref[tile * TILE] // 128 * 128, width - SPAN)
    end = cell_ref[tile * TILE + TILE - 1]
    cells = cells_ref[...]

    def picked(cells, start):
        start = pl.multiple_of(start, 128)
        pick = jnp.concatenate(
            [(cells == lane + (start + at)).astype(jnp.float32) for at in range(0, SPAN, 128)], axis=1
        ).astype(jnp.bfloat16)
        return dot(pick, states_ref[:, pl.ds(start, SPAN)], NT)

    acc_ref[...] = picked(cells, begin)

    def add(step, carry):
        lower = begin + step * SPAN
        acc_ref[...] += picked(
            jnp.where(cells >= lower, cells, -1), jnp.minimum(lower, width - SPAN)
        )
        return carry

    lax.fori_loop(1, (end - begin) // SPAN + 1, add, 0)
    done = (acc_ref[...] * weight_ref[:, 0:1]).astype(jnp.bfloat16)

    @pl.when(tile < half)
    def _():
        first_ref[...] = done

    @pl.when(tile >= half)
    def _():
        last_ref[...] = done


def project(obs_cell, cells, weight, states, piece):
    width = states.shape[1]
    members = states.shape[0] // PIECES
    obs = obs_cell.shape[0]
    half = obs // TILE // 2
    side = jax.ShapeDtypeStruct((obs // 2, members), jnp.bfloat16)
    return pl.pallas_call(
        project_kernel,
        grid_spec=pltpu.PrefetchScalarGridSpec(
            num_scalar_prefetch=1,
            grid=(obs // TILE,),
            in_specs=[
                pl.BlockSpec((TILE, 128), lambda i, c: (i, 0)),
                pl.BlockSpec((TILE, 128), lambda i, c: (i, 0)),
                pl.BlockSpec((members, width), lambda i, c: (piece, 0)),
            ],
            out_specs=(
                pl.BlockSpec((TILE, members), lambda i, c: (jnp.minimum(i, half - 1), 0)),
                pl.BlockSpec((TILE, members), lambda i, c: (jnp.maximum(i - half, 0), 0)),
            ),
            scratch_shapes=[pltpu.VMEM((TILE, members), jnp.float32)],
        ),
        out_shape=(side, side),
        cost_estimate=pl.CostEstimate(
            flops=2 * obs * members * SPAN, bytes_accessed=8 * obs * members, transcendentals=0
        ),
        name="project",
    )(obs_cell, cells, weight, states)


def gram_kernel(slot_ref, *refs):
    pieces, states_ref = refs[: 4 * PIECES], refs[4 * PIECES]
    columns_ref, gram_ref, moved_ref, landed_ref, rows_ref, picked_ref, sems = refs[4 * PIECES + 1 :]
    step = pl.program_id(0)
    edge, part = pieces[0].shape
    tiles = part // 128
    width = PIECES * tiles
    per_step, kslots, _ = gram_ref.shape

    @pl.when(step == 0)
    def _():
        copies = [
            pltpu.make_async_copy(piece, landed_ref.at[at], sems.at[at]) for at, piece in enumerate(pieces)
        ]
        order = [chunk * 4 + side for side in (1, 2, 0, 3) for chunk in range(PIECES)]
        for at in order:
            copies[at].start()
        rows_ref[4 * edge * width :, :] = jnp.zeros((width, 128), jnp.float32)
        for at in order:
            chunk, side = divmod(at, 4)
            copies[at].wait()

            def spread(turn, carry):
                start = pl.multiple_of(turn * SPREAD, SPREAD)
                for tile in range(tiles):
                    value = landed_ref[at, pl.ds(start, SPREAD), tile * 128 : (tile + 1) * 128]
                    row = (side * edge + start) * width + chunk * tiles + tile
                    rows_ref[pl.ds(row, SPREAD, stride=width), :] = value.astype(jnp.float32)
                return carry

            lax.fori_loop(0, edge // SPREAD, spread, 0)

    for j in range(per_step):
        for k in range(kslots):
            row = pl.multiple_of(slot_ref[(step * per_step + j) * kslots + k], width)
            picked_ref[j, k * width : (k + 1) * width, :] = rows_ref[pl.ds(row, width), :]
    for j in range(per_step):
        chosen = jnp.concatenate(
            [picked_ref[j, pl.ds(at, kslots, stride=width), :].astype(jnp.bfloat16) for at in range(width)],
            axis=1,
        )
        columns_ref[j] = chosen
        gram_ref[j] = dot(chosen, chosen, NT)
        cells = slice(j * 128, j * 128 + 128)
        moved_ref[j] = dot(chosen, states_ref[:, cells])


def gather_gram(slots, pieces, states, blocks, per_step=GRAM_STEP):
    members, width = states.shape
    edge, part = pieces[0].shape
    kslots = slots.shape[0] // blocks
    square = pl.BlockSpec((per_step, kslots, kslots), lambda i, s: (i, 0, 0))
    squares = jax.ShapeDtypeStruct((blocks, kslots, kslots), jnp.float32)
    lanes = members // 128
    return pl.pallas_call(
        gram_kernel,
        grid_spec=pltpu.PrefetchScalarGridSpec(
            num_scalar_prefetch=1,
            grid=(blocks // per_step,),
            in_specs=[pl.BlockSpec(memory_space=pl.ANY)] * len(pieces)
            + [pl.BlockSpec((members, per_step * width // blocks), lambda i, s: (0, i))],
            out_specs=(
                pl.BlockSpec((per_step, kslots, members), lambda i, s: (i, 0, 0)),
                square,
                square,
            ),
            scratch_shapes=[
                pltpu.VMEM((len(pieces), edge, part), jnp.bfloat16),
                pltpu.VMEM(((4 * edge + 1) * lanes, 128), jnp.float32),
                pltpu.VMEM((per_step, kslots * lanes, 128), jnp.float32),
                pltpu.SemaphoreType.DMA((len(pieces),)),
            ],
        ),
        out_shape=(jax.ShapeDtypeStruct((blocks, kslots, members), jnp.bfloat16), squares, squares),
        compiler_params=pltpu.CompilerParams(vmem_limit_bytes=60 * 1024 * 1024),
        cost_estimate=pl.CostEstimate(
            flops=4 * blocks * kslots * kslots * members,
            bytes_accessed=16 * members * width,
            transcendentals=0,
        ),
        name="gather_gram",
    )(slots, *pieces, states)


def three_way(v):
    hi = v.astype(jnp.bfloat16)
    rest = v - hi.astype(jnp.float32)
    mid = rest.astype(jnp.bfloat16)
    low = (rest - mid.astype(jnp.float32)).astype(jnp.bfloat16)
    return hi, mid, low


def invert_kernel(gram_ref, out_ref, work):
    nblk, n, _ = gram_ref.shape
    lane = lax.broadcasted_iota(jnp.int32, (8, n), 1)
    sub = lax.broadcasted_iota(jnp.int32, (8, n), 0)
    lane2 = lax.broadcasted_iota(jnp.int32, (1, n), 1)
    rows = lax.broadcasted_iota(jnp.int32, (1, n, n), 1)
    cols = lax.broadcasted_iota(jnp.int32, (1, n, n), 2)
    work[...] = gram_ref[...] + jnp.where(rows == cols, 1.0, 0.0)

    def step(number, carry):
        flip = lane2 >= n - number * NB
        panel = [[work[b, at : at + 8, :] for at in range(0, NB, 8)] for b in range(nblk)]
        for k in range(NB):
            here = lane == k
            own, at = divmod(k, 8)
            for b in range(nblk):
                col = [jnp.broadcast_to(p[:, k : k + 1], (8, n)) for p in panel[b]]
                inv = 1.0 / col[own][at : at + 1, :]
                scaled = jnp.where(here[0:1], inv, panel[b][own][at : at + 1, :] * inv)
                scaled = jnp.broadcast_to(scaled, (8, n))
                new = [jnp.where(here, 0.0, p) - c * scaled for p, c in zip(panel[b], col)]
                new[own] = jnp.where(sub == at, scaled, new[own])
                panel[b] = new
        for b in range(nblk):
            sides = work[b, 0:NB, :]
            sides = jnp.where(flip, -sides, sides)
            rolled = pltpu.roll(jnp.concatenate(panel[b], axis=0), n - NB, 1)
            rh, rm, rl = three_way(rolled)
            ch, cm, cl = three_way(sides)
            rhs = jnp.concatenate([rh, rm, rh, rl, rm, rh, rl, rm], axis=0)
            lhs = jnp.concatenate([ch, ch, cm, ch, cm, cl, cm, cl], axis=0)
            change = dot(lhs, rhs, TN)
            kept = pltpu.roll(jnp.where(lane2 < NB, 0.0, work[b, NB:n, :]), n - NB, 1)
            work[b, 0 : n - NB, :] = kept - change[NB:n]
            work[b, n - NB : n, :] = rolled
        return carry

    lax.fori_loop(0, n // NB, step, 0)
    out_ref[...] = work[...]


def invert(gram):
    return pl.pallas_call(
        invert_kernel,
        out_shape=jax.ShapeDtypeStruct(gram.shape, jnp.float32),
        scratch_shapes=[pltpu.VMEM(gram.shape, jnp.float32)],
        name="invert_blocks",
    )(gram)


def update_kernel(inverse_ref, moved_ref, columns_ref, states_ref, out_ref):
    groups, rows, _ = out_ref.shape
    for at in range(inverse_ref.shape[0]):
        wh, wm, wl = three_way(inverse_ref[at])
        mh, mm, ml = three_way(moved_ref[at] * 0.5)
        solved = dot(
            jnp.concatenate([wh, wh, wm, wh, wl, wm], axis=1),
            jnp.concatenate([mh, mm, mh, ml, mh, mm], axis=0),
        )
        high = solved.astype(jnp.bfloat16)
        low = (solved - high.astype(jnp.float32)).astype(jnp.bfloat16)
        columns = columns_ref[at].T
        change = dot(
            jnp.concatenate([columns, columns], axis=1), jnp.concatenate([high, low], axis=0)
        )
        cells = slice(at * 128, at * 128 + 128)
        updated = (states_ref[:, cells].astype(jnp.float32) - change).astype(jnp.bfloat16)
        out_ref[:, :, cells] = updated.reshape(groups, rows, 128)


def update(inverse, moved, columns, states, groups, per_step=4):
    blocks, kslots, _ = inverse.shape
    square = pl.BlockSpec((per_step, kslots, kslots), lambda i: (i, 0, 0))
    members, width = states.shape
    return pl.pallas_call(
        update_kernel,
        grid=(blocks // per_step,),
        in_specs=[
            square,
            square,
            pl.BlockSpec((per_step, kslots, members), lambda i: (i, 0, 0)),
            pl.BlockSpec((members, per_step * kslots), lambda i: (0, i)),
        ],
        out_specs=pl.BlockSpec((groups, members // groups, per_step * kslots), lambda i: (0, 0, i)),
        out_shape=jax.ShapeDtypeStruct((groups, members // groups, width), jnp.bfloat16),
        name="update",
    )(inverse, moved, columns, states)


def on_device(deviations, obs_cell, obs_weight, block_obs, block_count):
    groups = lax.axis_size("mem")
    members = deviations.shape[0] * groups
    obs_dev = obs_cell.shape[0]
    weight = obs_weight * (1.0 / math.sqrt(members - 1))
    cells = jnp.broadcast_to(obs_cell[:, None], (obs_dev, 128))
    weights = jnp.broadcast_to(weight[:, None], (obs_dev, 128))
    line_index = lax.axis_index("space") * groups + lax.axis_index("mem")
    local_index = block_obs - (line_index * obs_dev - obs_dev // 2)
    slot_ids = jnp.arange(block_obs.shape[1], dtype=jnp.int32)
    slots = jnp.where(slot_ids[None, :] < block_count[:, None], local_index, 2 * obs_dev)
    slots = slots.reshape(-1) * (members // 128)
    size = lax.axis_size("space") * groups
    up = [(i, i + 1) for i in range(size - 1)]
    down = [(b, a) for a, b in up]
    states = lax.all_to_all(deviations, "mem", split_axis=1, concat_axis=0, tiled=True)
    pieces = []
    for piece in range(PIECES):
        first, last = project(obs_cell, cells, weights, states, piece)
        low = lax.ppermute(last, ("space", "mem"), up)
        high = lax.ppermute(first, ("space", "mem"), down)
        pieces += [low, first, last, high]
    columns, gram, moved = gather_gram(slots, pieces, states, block_obs.shape[0])
    analysis = update(invert(gram), moved, columns, states, groups)
    return lax.all_to_all(
        analysis.reshape(members, -1), "mem", split_axis=0, concat_axis=1, tiled=True
    )


def solution(mesh):
    in_specs = (
        P("mem", "space"),
        P(("space", "mem")),
        P(("space", "mem")),
        P(("space", "mem"), None),
        P(("space", "mem")),
    )
    out_specs = P("mem", "space")

    return jax.shard_map(
        on_device, mesh=mesh, in_specs=in_specs, out_specs=out_specs, check_vma=False
    )
```

```python
import math

import jax
import jax.numpy as jnp
from jax import lax
from jax.experimental import pallas as pl
from jax.experimental.pallas import tpu as pltpu
from jax.sharding import PartitionSpec as P


NB = 16
TILE = 512
PIECES = 2
SUB = 256
SPAN = 512
GRAM_STEP = 4
SPREAD = 64

NT = (((1,), (1,)), ((), ()))
TN = (((0,), (0,)), ((), ()))


def dot(a, b, dims=(((1,), (0,)), ((), ())), precision=None):
    return lax.dot_general(a, b, dims, precision=precision, preferred_element_type=jnp.float32)


def project_kernel(cell_ref, lists_ref, states_ref, first_ref, last_ref, acc_ref):
    tile = pl.program_id(0)
    half = pl.num_programs(0) // 2
    width = states_ref.shape[1]
    lane = lax.broadcasted_iota(jnp.int32, (TILE, 128), 1).astype(jnp.float32)
    parts = TILE // 128
    upright = lists_ref[0].T

    def column(at):
        return jnp.concatenate(
            [jnp.broadcast_to(upright[:, at + k : at + k + 1], (128, 128)) for k in range(parts)], axis=0
        )

    beyond = column(0) - lane
    weights = column(parts)
    members = states_ref.shape[0]

    def picked(beyond, start):
        start = pl.multiple_of(start, 128)
        base = start.astype(jnp.float32)
        pick = jnp.concatenate(
            [(beyond == base + at).astype(jnp.float32) for at in range(0, SPAN, 128)], axis=1
        ).astype(jnp.bfloat16)
        return dot(pick, states_ref[:, pl.ds(start, SPAN)], NT)

    def scaled(values, weights):
        return (values * jnp.concatenate([weights] * (members // 128), axis=1)).astype(jnp.bfloat16)

    for sub in range(0, TILE, SUB):
        rows = slice(sub, sub + SUB)
        begin = jnp.minimum(cell_ref[tile * TILE + sub] // 128 * 128, width - SPAN)
        end = cell_ref[tile * TILE + sub + SUB - 1]
        last_ref[rows] = scaled(picked(beyond[rows], begin), weights[rows])

        @pl.when(end >= begin + SPAN)
        def _():
            acc_ref[...] = picked(beyond[rows], begin)

            def add(step, carry):
                lower = begin + step * SPAN
                own = jnp.where(
                    beyond[rows] + lane[rows] >= lower.astype(jnp.float32), beyond[rows], -2.0 * width
                )
                acc_ref[...] += picked(own, jnp.minimum(lower, width - SPAN))
                return carry

            lax.fori_loop(1, (end - begin) // SPAN + 1, add, 0)
            last_ref[rows] = scaled(acc_ref[...], weights[rows])

    @pl.when(tile < half)
    def _():
        first_ref[...] = last_ref[...]


def project(obs_cell, lists, states, piece):
    width = states.shape[1]
    members = states.shape[0] // PIECES
    obs = obs_cell.shape[0]
    half = obs // TILE // 2
    side = jax.ShapeDtypeStruct((obs // 2, members), jnp.bfloat16)
    return pl.pallas_call(
        project_kernel,
        grid_spec=pltpu.PrefetchScalarGridSpec(
            num_scalar_prefetch=1,
            grid=(obs // TILE,),
            in_specs=[
                pl.BlockSpec((1, 2 * TILE // 128, 128), lambda i, c: (i, 0, 0)),
                pl.BlockSpec((members, width), lambda i, c: (piece, 0)),
            ],
            out_specs=(
                pl.BlockSpec((TILE, members), lambda i, c: (jnp.minimum(i, half - 1), 0)),
                pl.BlockSpec((TILE, members), lambda i, c: (jnp.maximum(i - half, 0), 0)),
            ),
            scratch_shapes=[pltpu.VMEM((SUB, members), jnp.float32)],
        ),
        out_shape=(side, side),
        compiler_params=pltpu.CompilerParams(vmem_limit_bytes=16 * 1024 * 1024),
        cost_estimate=pl.CostEstimate(
            flops=2 * obs * members * SPAN, bytes_accessed=8 * obs * members, transcendentals=0
        ),
        name="project",
    )(obs_cell, lists, states)


def gram_kernel(slot_ref, *refs):
    pieces, states_ref = refs[: 4 * PIECES], refs[4 * PIECES]
    columns_ref, gram_ref, moved_ref, landed_ref, rows_ref, picked_ref, sems = refs[4 * PIECES + 1 :]
    step = pl.program_id(0)
    edge, part = pieces[0].shape
    tiles = part // 128
    width = PIECES * tiles
    per_step, kslots, _ = gram_ref.shape

    @pl.when(step == 0)
    def _():
        copies = [
            pltpu.make_async_copy(piece, landed_ref.at[at], sems.at[at]) for at, piece in enumerate(pieces)
        ]
        order = [chunk * 4 + side for side in (1, 2, 0, 3) for chunk in range(PIECES)]
        for at in order:
            copies[at].start()
        rows_ref[4 * edge * width :, :] = jnp.zeros((width, 128), jnp.float32)
        for at in order:
            chunk, side = divmod(at, 4)
            copies[at].wait()

            def spread(turn, carry):
                start = pl.multiple_of(turn * SPREAD, SPREAD)
                for tile in range(tiles):
                    value = landed_ref[at, pl.ds(start, SPREAD), tile * 128 : (tile + 1) * 128]
                    row = (side * edge + start) * width + chunk * tiles + tile
                    rows_ref[pl.ds(row, SPREAD, stride=width), :] = value.astype(jnp.float32)
                return carry

            lax.fori_loop(0, edge // SPREAD, spread, 0)

    for j in range(per_step):
        for k in range(kslots):
            row = pl.multiple_of(slot_ref[(step * per_step + j) * kslots + k], width)
            picked_ref[j, k * width : (k + 1) * width, :] = rows_ref[pl.ds(row, width), :]
    for j in range(per_step):
        chosen = jnp.concatenate(
            [picked_ref[j, pl.ds(at, kslots, stride=width), :].astype(jnp.bfloat16) for at in range(width)],
            axis=1,
        )
        columns_ref[j] = chosen
        gram_ref[j] = dot(chosen, chosen, NT)
        cells = slice(j * 128, j * 128 + 128)
        moved_ref[j] = dot(chosen, states_ref[:, cells])


def gather_gram(slots, pieces, states, blocks, per_step=GRAM_STEP):
    members, width = states.shape
    edge, part = pieces[0].shape
    kslots = slots.shape[0] // blocks
    square = pl.BlockSpec((per_step, kslots, kslots), lambda i, s: (i, 0, 0))
    squares = jax.ShapeDtypeStruct((blocks, kslots, kslots), jnp.float32)
    lanes = members // 128
    return pl.pallas_call(
        gram_kernel,
        grid_spec=pltpu.PrefetchScalarGridSpec(
            num_scalar_prefetch=1,
            grid=(blocks // per_step,),
            in_specs=[pl.BlockSpec(memory_space=pl.ANY)] * len(pieces)
            + [pl.BlockSpec((members, per_step * width // blocks), lambda i, s: (0, i))],
            out_specs=(
                pl.BlockSpec((per_step, kslots, members), lambda i, s: (i, 0, 0)),
                square,
                square,
            ),
            scratch_shapes=[
                pltpu.VMEM((len(pieces), edge, part), jnp.bfloat16),
                pltpu.VMEM(((4 * edge + 1) * lanes, 128), jnp.float32),
                pltpu.VMEM((per_step, kslots * lanes, 128), jnp.float32),
                pltpu.SemaphoreType.DMA((len(pieces),)),
            ],
        ),
        out_shape=(jax.ShapeDtypeStruct((blocks, kslots, members), jnp.bfloat16), squares, squares),
        compiler_params=pltpu.CompilerParams(vmem_limit_bytes=38 * 1024 * 1024),
        cost_estimate=pl.CostEstimate(
            flops=4 * blocks * kslots * kslots * members,
            bytes_accessed=16 * members * width,
            transcendentals=0,
        ),
        name="gather_gram",
    )(slots, *pieces, states)


def three_way(v):
    hi = v.astype(jnp.bfloat16)
    rest = v - hi.astype(jnp.float32)
    mid = rest.astype(jnp.bfloat16)
    low = (rest - mid.astype(jnp.float32)).astype(jnp.bfloat16)
    return hi, mid, low


def invert_kernel(gram_ref, out_ref, work):
    nblk, n, _ = gram_ref.shape
    lane = lax.broadcasted_iota(jnp.int32, (8, n), 1)
    sub = lax.broadcasted_iota(jnp.int32, (8, n), 0)
    lane2 = lax.broadcasted_iota(jnp.int32, (1, n), 1)
    rows = lax.broadcasted_iota(jnp.int32, (1, n, n), 1)
    cols = lax.broadcasted_iota(jnp.int32, (1, n, n), 2)
    work[...] = gram_ref[...] + jnp.where(rows == cols, 1.0, 0.0)

    def step(number, carry):
        flip = lane2 >= n - number * NB
        panel = [[work[b, at : at + 8, :] for at in range(0, NB, 8)] for b in range(nblk)]
        for k in range(NB):
            here = lane == k
            own, at = divmod(k, 8)
            for b in range(nblk):
                col = [jnp.broadcast_to(p[:, k : k + 1], (8, n)) for p in panel[b]]
                inv = 1.0 / col[own][at : at + 1, :]
                scaled = jnp.where(here[0:1], inv, panel[b][own][at : at + 1, :] * inv)
                scaled = jnp.broadcast_to(scaled, (8, n))
                new = [jnp.where(here, 0.0, p) - c * scaled for p, c in zip(panel[b], col)]
                new[own] = jnp.where(sub == at, scaled, new[own])
                panel[b] = new
        for b in range(nblk):
            sides = work[b, 0:NB, :]
            sides = jnp.where(flip, -sides, sides)
            rolled = pltpu.roll(jnp.concatenate(panel[b], axis=0), n - NB, 1)
            rh, rm, rl = three_way(rolled)
            ch, cm, cl = three_way(sides)
            rhs = jnp.concatenate([rh, rm, rh, rl, rm, rh, rl, rm], axis=0)
            lhs = jnp.concatenate([ch, ch, cm, ch, cm, cl, cm, cl], axis=0)
            change = dot(lhs, rhs, TN)
            kept = pltpu.roll(jnp.where(lane2 < NB, 0.0, work[b, NB:n, :]), n - NB, 1)
            work[b, 0 : n - NB, :] = kept - change[NB:n]
            work[b, n - NB : n, :] = rolled
        return carry

    lax.fori_loop(0, n // NB, step, 0)
    out_ref[...] = work[...]


def invert(gram):
    return pl.pallas_call(
        invert_kernel,
        out_shape=jax.ShapeDtypeStruct(gram.shape, jnp.float32),
        scratch_shapes=[pltpu.VMEM(gram.shape, jnp.float32)],
        compiler_params=pltpu.CompilerParams(vmem_limit_bytes=10 * 1024 * 1024),
        name="invert_blocks",
    )(gram)


def update_kernel(inverse_ref, moved_ref, columns_ref, states_ref, out_ref):
    groups, rows, _ = out_ref.shape
    for at in range(inverse_ref.shape[0]):
        wh, wm, wl = three_way(inverse_ref[at])
        mh, mm, ml = three_way(moved_ref[at] * 0.5)
        solved = dot(
            jnp.concatenate([wh, wh, wm, wh, wl, wm], axis=1),
            jnp.concatenate([mh, mm, mh, ml, mh, mm], axis=0),
        )
        high = solved.astype(jnp.bfloat16)
        low = (solved - high.astype(jnp.float32)).astype(jnp.bfloat16)
        columns = columns_ref[at].T
        change = dot(
            jnp.concatenate([columns, columns], axis=1), jnp.concatenate([high, low], axis=0)
        )
        cells = slice(at * 128, at * 128 + 128)
        updated = (states_ref[:, cells].astype(jnp.float32) - change).astype(jnp.bfloat16)
        out_ref[:, :, cells] = updated.reshape(groups, rows, 128)


def update(inverse, moved, columns, states, groups, per_step=4):
    blocks, kslots, _ = inverse.shape
    square = pl.BlockSpec((per_step, kslots, kslots), lambda i: (i, 0, 0))
    members, width = states.shape
    return pl.pallas_call(
        update_kernel,
        grid=(blocks // per_step,),
        in_specs=[
            square,
            square,
            pl.BlockSpec((per_step, kslots, members), lambda i: (i, 0, 0)),
            pl.BlockSpec((members, per_step * kslots), lambda i: (0, i)),
        ],
        out_specs=pl.BlockSpec((groups, members // groups, per_step * kslots), lambda i: (0, 0, i)),
        out_shape=jax.ShapeDtypeStruct((groups, members // groups, width), jnp.bfloat16),
        compiler_params=pltpu.CompilerParams(vmem_limit_bytes=24 * 1024 * 1024),
        name="update",
    )(inverse, moved, columns, states)


def on_device(deviations, obs_cell, obs_weight, block_obs, block_count):
    groups = lax.axis_size("mem")
    members = deviations.shape[0] * groups
    obs_dev = obs_cell.shape[0]
    weight = obs_weight * (1.0 / math.sqrt(members - 1))
    lists = jnp.concatenate(
        [v.reshape(-1, TILE // 128, 128) for v in (obs_cell.astype(jnp.float32), weight)], axis=1
    )
    line_index = lax.axis_index("space") * groups + lax.axis_index("mem")
    local_index = block_obs - (line_index * obs_dev - obs_dev // 2)
    slot_ids = jnp.arange(block_obs.shape[1], dtype=jnp.int32)
    slots = jnp.where(slot_ids[None, :] < block_count[:, None], local_index, 2 * obs_dev)
    slots = slots.reshape(-1) * (members // 128)
    size = lax.axis_size("space") * groups
    up = [(i, i + 1) for i in range(size - 1)]
    down = [(b, a) for a, b in up]
    states = lax.all_to_all(deviations, "mem", split_axis=1, concat_axis=0, tiled=True)
    pieces = []
    for piece in range(PIECES):
        first, last = project(obs_cell, lists, states, piece)
        low = lax.ppermute(last, ("space", "mem"), up)
        high = lax.ppermute(first, ("space", "mem"), down)
        pieces += [low, first, last, high]
    columns, gram, moved = gather_gram(slots, pieces, states, block_obs.shape[0])
    analysis = update(invert(gram), moved, columns, states, groups)
    return lax.all_to_all(
        analysis.reshape(members, -1), "mem", split_axis=0, concat_axis=1, tiled=True
    )


def solution(mesh):
    in_specs = (
        P("mem", "space"),
        P(("space", "mem")),
        P(("space", "mem")),
        P(("space", "mem"), None),
        P(("space", "mem")),
    )
    out_specs = P("mem", "space")

    return jax.shard_map(
        on_device, mesh=mesh, in_specs=in_specs, out_specs=out_specs, check_vma=False
    )
```

```python
import math

import jax
import jax.numpy as jnp
from jax import lax
from jax.experimental import pallas as pl
from jax.experimental.pallas import tpu as pltpu
from jax.sharding import PartitionSpec as P


NB = 16
TILE = 512
PIECES = 2
SUB = 256
SPAN = 512
GRAM_STEP = 4
SPREAD = 64

NT = (((1,), (1,)), ((), ()))
TN = (((0,), (0,)), ((), ()))


def dot(a, b, dims=(((1,), (0,)), ((), ())), precision=None):
    return lax.dot_general(a, b, dims, precision=precision, preferred_element_type=jnp.float32)


def project_kernel(cell_ref, lists_ref, states_ref, first_ref, last_ref, acc_ref):
    tile = pl.program_id(0)
    half = pl.num_programs(0) // 2
    width = states_ref.shape[1]
    lane = lax.broadcasted_iota(jnp.int32, (TILE, 128), 1).astype(jnp.float32)
    parts = TILE // 128
    upright = lists_ref[0].T

    def column(at):
        return jnp.concatenate(
            [jnp.broadcast_to(upright[:, at + k : at + k + 1], (128, 128)) for k in range(parts)], axis=0
        )

    beyond = column(0) - lane
    weights = column(parts)
    members = states_ref.shape[0]

    def picked(beyond, start):
        start = pl.multiple_of(start, 128)
        base = start.astype(jnp.float32)
        pick = jnp.concatenate(
            [(beyond == base + at).astype(jnp.float32) for at in range(0, SPAN, 128)], axis=1
        ).astype(jnp.bfloat16)
        return dot(pick, states_ref[:, pl.ds(start, SPAN)], NT)

    def scaled(values, weights):
        return (values * jnp.concatenate([weights] * (members // 128), axis=1)).astype(jnp.bfloat16)

    for sub in range(0, TILE, SUB):
        rows = slice(sub, sub + SUB)
        begin = jnp.minimum(cell_ref[tile * TILE + sub] // 128 * 128, width - SPAN)
        end = cell_ref[tile * TILE + sub + SUB - 1]
        last_ref[rows] = scaled(picked(beyond[rows], begin), weights[rows])

        @pl.when(end >= begin + SPAN)
        def _():
            acc_ref[...] = picked(beyond[rows], begin)

            def add(step, carry):
                lower = begin + step * SPAN
                own = jnp.where(
                    beyond[rows] + lane[rows] >= lower.astype(jnp.float32), beyond[rows], -2.0 * width
                )
                acc_ref[...] += picked(own, jnp.minimum(lower, width - SPAN))
                return carry

            lax.fori_loop(1, (end - begin) // SPAN + 1, add, 0)
            last_ref[rows] = scaled(acc_ref[...], weights[rows])

    @pl.when(tile < half)
    def _():
        first_ref[...] = last_ref[...]


def project(obs_cell, lists, states, piece):
    width = states.shape[1]
    members = states.shape[0] // PIECES
    obs = obs_cell.shape[0]
    half = obs // TILE // 2
    side = jax.ShapeDtypeStruct((obs // 2, members), jnp.bfloat16)
    return pl.pallas_call(
        project_kernel,
        grid_spec=pltpu.PrefetchScalarGridSpec(
            num_scalar_prefetch=1,
            grid=(obs // TILE,),
            in_specs=[
                pl.BlockSpec((1, 2 * TILE // 128, 128), lambda i, c: (i, 0, 0)),
                pl.BlockSpec((members, width), lambda i, c: (piece, 0)),
            ],
            out_specs=(
                pl.BlockSpec((TILE, members), lambda i, c: (jnp.minimum(i, half - 1), 0)),
                pl.BlockSpec((TILE, members), lambda i, c: (jnp.maximum(i - half, 0), 0)),
            ),
            scratch_shapes=[pltpu.VMEM((SUB, members), jnp.float32)],
        ),
        out_shape=(side, side),
        compiler_params=pltpu.CompilerParams(vmem_limit_bytes=16 * 1024 * 1024),
        cost_estimate=pl.CostEstimate(
            flops=2 * obs * members * SPAN, bytes_accessed=8 * obs * members, transcendentals=0
        ),
        name="project",
    )(obs_cell, lists, states)


def gram_kernel(slot_ref, *refs):
    pieces, states_ref = refs[: 4 * PIECES], refs[4 * PIECES]
    columns_ref, gram_ref, moved_ref, landed_ref, rows_ref, picked_ref, sems = refs[4 * PIECES + 1 :]
    step = pl.program_id(0)
    edge, part = pieces[0].shape
    tiles = part // 128
    width = PIECES * tiles
    per_step, kslots, _ = gram_ref.shape

    @pl.when(step == 0)
    def _():
        copies = [
            pltpu.make_async_copy(piece, landed_ref.at[at], sems.at[at]) for at, piece in enumerate(pieces)
        ]
        order = [chunk * 4 + side for side in (1, 2, 0, 3) for chunk in range(PIECES)]
        for at in order:
            copies[at].start()
        rows_ref[4 * edge * width :, :] = jnp.zeros((width, 128), jnp.float32)
        for at in order:
            chunk, side = divmod(at, 4)
            copies[at].wait()

            def spread(turn, carry):
                start = pl.multiple_of(turn * SPREAD, SPREAD)
                for tile in range(tiles):
                    value = landed_ref[at, pl.ds(start, SPREAD), tile * 128 : (tile + 1) * 128]
                    row = (side * edge + start) * width + chunk * tiles + tile
                    rows_ref[pl.ds(row, SPREAD, stride=width), :] = value.astype(jnp.float32)
                return carry

            lax.fori_loop(0, edge // SPREAD, spread, 0)

    for j in range(per_step):
        for k in range(kslots):
            row = pl.multiple_of(slot_ref[(step * per_step + j) * kslots + k], width)
            picked_ref[j, k * width : (k + 1) * width, :] = rows_ref[pl.ds(row, width), :]
    for j in range(per_step):
        chosen = jnp.concatenate(
            [picked_ref[j, pl.ds(at, kslots, stride=width), :].astype(jnp.bfloat16) for at in range(width)],
            axis=1,
        )
        columns_ref[j] = chosen
        gram_ref[j] = dot(chosen, chosen, NT)
        cells = slice(j * 128, j * 128 + 128)
        moved_ref[j] = dot(chosen, states_ref[:, cells])


def gather_gram(slots, pieces, states, blocks, per_step=GRAM_STEP):
    members, width = states.shape
    edge, part = pieces[0].shape
    kslots = slots.shape[0] // blocks
    square = pl.BlockSpec((per_step, kslots, kslots), lambda i, s: (i, 0, 0))
    squares = jax.ShapeDtypeStruct((blocks, kslots, kslots), jnp.float32)
    lanes = members // 128
    return pl.pallas_call(
        gram_kernel,
        grid_spec=pltpu.PrefetchScalarGridSpec(
            num_scalar_prefetch=1,
            grid=(blocks // per_step,),
            in_specs=[pl.BlockSpec(memory_space=pl.ANY)] * len(pieces)
            + [pl.BlockSpec((members, per_step * width // blocks), lambda i, s: (0, i))],
            out_specs=(
                pl.BlockSpec((per_step, kslots, members), lambda i, s: (i, 0, 0)),
                square,
                square,
            ),
            scratch_shapes=[
                pltpu.VMEM((len(pieces), edge, part), jnp.bfloat16),
                pltpu.VMEM(((4 * edge + 1) * lanes, 128), jnp.float32),
                pltpu.VMEM((per_step, kslots * lanes, 128), jnp.float32),
                pltpu.SemaphoreType.DMA((len(pieces),)),
            ],
        ),
        out_shape=(jax.ShapeDtypeStruct((blocks, kslots, members), jnp.bfloat16), squares, squares),
        compiler_params=pltpu.CompilerParams(vmem_limit_bytes=38 * 1024 * 1024),
        cost_estimate=pl.CostEstimate(
            flops=4 * blocks * kslots * kslots * members,
            bytes_accessed=16 * members * width,
            transcendentals=0,
        ),
        name="gather_gram",
    )(slots, *pieces, states)


def three_way(v):
    hi = v.astype(jnp.bfloat16)
    rest = v - hi.astype(jnp.float32)
    mid = rest.astype(jnp.bfloat16)
    low = (rest - mid.astype(jnp.float32)).astype(jnp.bfloat16)
    return hi, mid, low


def invert_kernel(gram_ref, out_ref, work):
    nblk, n, _ = gram_ref.shape
    lane = lax.broadcasted_iota(jnp.int32, (8, n), 1)
    sub = lax.broadcasted_iota(jnp.int32, (8, n), 0)
    lane2 = lax.broadcasted_iota(jnp.int32, (1, n), 1)
    rows = lax.broadcasted_iota(jnp.int32, (1, n, n), 1)
    cols = lax.broadcasted_iota(jnp.int32, (1, n, n), 2)
    work[...] = gram_ref[...] + jnp.where(rows == cols, 1.0, 0.0)

    for start in range(0, n, NB):
        panel = [[work[b, at : at + 8, :] for at in range(start, start + NB, 8)] for b in range(nblk)]
        for k in range(NB):
            here = lane == start + k
            own, at = divmod(k, 8)
            for b in range(nblk):
                col = [jnp.broadcast_to(p[:, start + k : start + k + 1], (8, n)) for p in panel[b]]
                inv = 1.0 / col[own][at : at + 1, :]
                scaled = jnp.where(here[0:1], inv, panel[b][own][at : at + 1, :] * inv)
                scaled = jnp.broadcast_to(scaled, (8, n))
                new = [jnp.where(here, 0.0, p) - c * scaled for p, c in zip(panel[b], col)]
                new[own] = jnp.where(sub == at, scaled, new[own])
                panel[b] = new
        inside = (lane2 >= start) & (lane2 < start + NB)
        for b in range(nblk):
            sides = work[b, start : start + NB, :]
            sides = jnp.where(lane2 < start, -sides, sides)
            done = jnp.concatenate(panel[b], axis=0)
            rh, rm, rl = three_way(done)
            ch, cm, cl = three_way(sides)
            rhs = jnp.concatenate([rh, rm, rh, rl, rm, rh, rl, rm], axis=0)
            lhs = jnp.concatenate([ch, ch, cm, ch, cm, cl, cm, cl], axis=0)
            change = dot(lhs, rhs, TN)
            for rows_at, count in ((0, start), (start + NB, n - NB - start)):
                if count:
                    rows = slice(rows_at, rows_at + count)
                    work[b, rows, :] = jnp.where(inside, 0.0, work[b, rows, :]) - change[rows]
            work[b, start : start + NB, :] = done

    out_ref[...] = work[...]


def invert(gram):
    return pl.pallas_call(
        invert_kernel,
        out_shape=jax.ShapeDtypeStruct(gram.shape, jnp.float32),
        scratch_shapes=[pltpu.VMEM(gram.shape, jnp.float32)],
        compiler_params=pltpu.CompilerParams(vmem_limit_bytes=10 * 1024 * 1024),
        name="invert_blocks",
    )(gram)


def update_kernel(inverse_ref, moved_ref, columns_ref, states_ref, out_ref):
    groups, rows, _ = out_ref.shape
    for at in range(inverse_ref.shape[0]):
        wh, wm, wl = three_way(inverse_ref[at])
        mh, mm, ml = three_way(moved_ref[at] * 0.5)
        solved = dot(
            jnp.concatenate([wh, wh, wm, wh, wl, wm], axis=1),
            jnp.concatenate([mh, mm, mh, ml, mh, mm], axis=0),
        )
        high = solved.astype(jnp.bfloat16)
        low = (solved - high.astype(jnp.float32)).astype(jnp.bfloat16)
        columns = columns_ref[at].T
        change = dot(
            jnp.concatenate([columns, columns], axis=1), jnp.concatenate([high, low], axis=0)
        )
        cells = slice(at * 128, at * 128 + 128)
        updated = (states_ref[:, cells].astype(jnp.float32) - change).astype(jnp.bfloat16)
        out_ref[:, :, cells] = updated.reshape(groups, rows, 128)


def update(inverse, moved, columns, states, groups, per_step=4):
    blocks, kslots, _ = inverse.shape
    square = pl.BlockSpec((per_step, kslots, kslots), lambda i: (i, 0, 0))
    members, width = states.shape
    return pl.pallas_call(
        update_kernel,
        grid=(blocks // per_step,),
        in_specs=[
            square,
            square,
            pl.BlockSpec((per_step, kslots, members), lambda i: (i, 0, 0)),
            pl.BlockSpec((members, per_step * kslots), lambda i: (0, i)),
        ],
        out_specs=pl.BlockSpec((groups, members // groups, per_step * kslots), lambda i: (0, 0, i)),
        out_shape=jax.ShapeDtypeStruct((groups, members // groups, width), jnp.bfloat16),
        compiler_params=pltpu.CompilerParams(vmem_limit_bytes=24 * 1024 * 1024),
        name="update",
    )(inverse, moved, columns, states)


def on_device(deviations, obs_cell, obs_weight, block_obs, block_count):
    groups = lax.axis_size("mem")
    members = deviations.shape[0] * groups
    obs_dev = obs_cell.shape[0]
    weight = obs_weight * (1.0 / math.sqrt(members - 1))
    lists = jnp.concatenate([v.reshape(-1, TILE // 128, 128) for v in (obs_cell.astype(jnp.float32), weight)], axis=1)
    line_index = lax.axis_index("space") * groups + lax.axis_index("mem")
    local_index = block_obs - (line_index * obs_dev - obs_dev // 2)
    slot_ids = jnp.arange(block_obs.shape[1], dtype=jnp.int32)
    slots = jnp.where(slot_ids[None, :] < block_count[:, None], local_index, 2 * obs_dev)
    slots = slots.reshape(-1) * (members // 128)
    size = lax.axis_size("space") * groups
    up = [(i, i + 1) for i in range(size - 1)]
    down = [(b, a) for a, b in up]
    deviations, lists = lax.optimization_barrier((deviations, lists))
    states = lax.all_to_all(deviations, "mem", split_axis=1, concat_axis=0, tiled=True)
    pieces = []
    for piece in range(PIECES):
        first, last = project(obs_cell, lists, states, piece)
        low = lax.ppermute(last, ("space", "mem"), up)
        high = lax.ppermute(first, ("space", "mem"), down)
        pieces += [low, first, last, high]
    columns, gram, moved = gather_gram(slots, pieces, states, block_obs.shape[0])
    analysis = update(invert(gram), moved, columns, states, groups)
    return lax.all_to_all(
        analysis.reshape(members, -1), "mem", split_axis=0, concat_axis=1, tiled=True
    )


def solution(mesh):
    in_specs = (
        P("mem", "space"),
        P(("space", "mem")),
        P(("space", "mem")),
        P(("space", "mem"), None),
        P(("space", "mem")),
    )
    out_specs = P("mem", "space")

    return jax.shard_map(on_device, mesh=mesh, in_specs=in_specs, out_specs=out_specs, check_vma=False)
```

```python
import functools
import math

import jax
import jax.numpy as jnp
from jax import lax
from jax.experimental import pallas as pl
from jax.experimental.pallas import tpu as pltpu
from jax.sharding import PartitionSpec as P


NB = 16
TILE = 512
PIECES = 2
SUB = 256
SPAN = 512
GRAM_STEP = 4
SPREAD = 64

NT = (((1,), (1,)), ((), ()))
TN = (((0,), (0,)), ((), ()))


def dot(a, b, dims=(((1,), (0,)), ((), ())), precision=None):
    return lax.dot_general(a, b, dims, precision=precision, preferred_element_type=jnp.float32)


def project_kernel(cell_ref, cells_ref, weights_ref, states_ref, first_ref, last_ref, acc_ref, *, scale):
    tile = pl.program_id(0)
    half = pl.num_programs(0) // 2
    width = states_ref.shape[1]
    lane = lax.broadcasted_iota(jnp.int32, (TILE, 128), 1).astype(jnp.float32)
    parts = TILE // 128
    upright = jnp.concatenate([cells_ref[0].astype(jnp.float32), weights_ref[0] * scale], axis=0).T

    def column(at):
        return jnp.concatenate(
            [jnp.broadcast_to(upright[:, at + k : at + k + 1], (128, 128)) for k in range(parts)], axis=0
        )

    beyond = column(0) - lane
    weights = column(parts)
    members = states_ref.shape[0]

    def picked(beyond, start):
        start = pl.multiple_of(start, 128)
        base = start.astype(jnp.float32)
        pick = jnp.concatenate(
            [(beyond == base + at).astype(jnp.float32) for at in range(0, SPAN, 128)], axis=1
        ).astype(jnp.bfloat16)
        return dot(pick, states_ref[:, pl.ds(start, SPAN)], NT)

    def scaled(values, weights):
        return (values * jnp.concatenate([weights] * (members // 128), axis=1)).astype(jnp.bfloat16)

    for sub in range(0, TILE, SUB):
        rows = slice(sub, sub + SUB)
        begin = jnp.minimum(cell_ref[tile * TILE + sub] // 128 * 128, width - SPAN)
        end = cell_ref[tile * TILE + sub + SUB - 1]
        last_ref[rows] = scaled(picked(beyond[rows], begin), weights[rows])

        @pl.when(end >= begin + SPAN)
        def _():
            acc_ref[...] = picked(beyond[rows], begin)

            def add(step, carry):
                lower = begin + step * SPAN
                own = jnp.where(
                    beyond[rows] + lane[rows] >= lower.astype(jnp.float32), beyond[rows], -2.0 * width
                )
                acc_ref[...] += picked(own, jnp.minimum(lower, width - SPAN))
                return carry

            lax.fori_loop(1, (end - begin) // SPAN + 1, add, 0)
            last_ref[rows] = scaled(acc_ref[...], weights[rows])

    @pl.when(tile < half)
    def _():
        first_ref[...] = last_ref[...]


def project(obs_cell, obs_weight, states, piece):
    lists = [v.reshape(-1, TILE // 128, 128) for v in (obs_cell, obs_weight)]
    scale = 1.0 / math.sqrt(states.shape[0] - 1)
    width = states.shape[1]
    members = states.shape[0] // PIECES
    obs = obs_cell.shape[0]
    half = obs // TILE // 2
    side = jax.ShapeDtypeStruct((obs // 2, members), jnp.bfloat16)
    return pl.pallas_call(
        functools.partial(project_kernel, scale=scale),
        grid_spec=pltpu.PrefetchScalarGridSpec(
            num_scalar_prefetch=1,
            grid=(obs // TILE,),
            in_specs=[
                pl.BlockSpec((1, TILE // 128, 128), lambda i, c: (i, 0, 0)),
                pl.BlockSpec((1, TILE // 128, 128), lambda i, c: (i, 0, 0)),
                pl.BlockSpec((members, width), lambda i, c: (piece, 0)),
            ],
            out_specs=(
                pl.BlockSpec((TILE, members), lambda i, c: (jnp.minimum(i, half - 1), 0)),
                pl.BlockSpec((TILE, members), lambda i, c: (jnp.maximum(i - half, 0), 0)),
            ),
            scratch_shapes=[pltpu.VMEM((SUB, members), jnp.float32)],
        ),
        out_shape=(side, side),
        compiler_params=pltpu.CompilerParams(vmem_limit_bytes=16 * 1024 * 1024),
        cost_estimate=pl.CostEstimate(
            flops=2 * obs * members * SPAN, bytes_accessed=8 * obs * members, transcendentals=0
        ),
        name="project",
    )(obs_cell, *lists, states)


def gram_kernel(slot_ref, *refs):
    pieces, states_ref = refs[: 4 * PIECES], refs[4 * PIECES]
    columns_ref, gram_ref, moved_ref, landed_ref, rows_ref, picked_ref, sems = refs[4 * PIECES + 1 :]
    step = pl.program_id(0)
    edge, part = pieces[0].shape
    tiles = part // 128
    width = PIECES * tiles
    per_step, kslots, _ = gram_ref.shape

    @pl.when(step == 0)
    def _():
        copies = [
            pltpu.make_async_copy(piece, landed_ref.at[at], sems.at[at]) for at, piece in enumerate(pieces)
        ]
        order = [chunk * 4 + side for side in (1, 2, 0, 3) for chunk in range(PIECES)]
        for at in order:
            copies[at].start()
        rows_ref[4 * edge * width :, :] = jnp.zeros((width, 128), jnp.float32)
        for at in order:
            chunk, side = divmod(at, 4)
            copies[at].wait()

            def spread(turn, carry):
                start = pl.multiple_of(turn * SPREAD, SPREAD)
                for tile in range(tiles):
                    value = landed_ref[at, pl.ds(start, SPREAD), tile * 128 : (tile + 1) * 128]
                    row = (side * edge + start) * width + chunk * tiles + tile
                    rows_ref[pl.ds(row, SPREAD, stride=width), :] = value.astype(jnp.float32)
                return carry

            lax.fori_loop(0, edge // SPREAD, spread, 0)

    for j in range(per_step):
        for k in range(kslots):
            row = pl.multiple_of(slot_ref[(step * per_step + j) * kslots + k], width)
            picked_ref[j, k * width : (k + 1) * width, :] = rows_ref[pl.ds(row, width), :]
    for j in range(per_step):
        chosen = jnp.concatenate(
            [picked_ref[j, pl.ds(at, kslots, stride=width), :].astype(jnp.bfloat16) for at in range(width)],
            axis=1,
        )
        columns_ref[j] = chosen
        gram_ref[j] = dot(chosen, chosen, NT)
        cells = slice(j * 128, j * 128 + 128)
        moved_ref[j] = dot(chosen, states_ref[:, cells])


def gather_gram(slots, pieces, states, blocks, per_step=GRAM_STEP):
    members, width = states.shape
    edge, part = pieces[0].shape
    kslots = slots.shape[0] // blocks
    square = pl.BlockSpec((per_step, kslots, kslots), lambda i, s: (i, 0, 0))
    squares = jax.ShapeDtypeStruct((blocks, kslots, kslots), jnp.float32)
    lanes = members // 128
    return pl.pallas_call(
        gram_kernel,
        grid_spec=pltpu.PrefetchScalarGridSpec(
            num_scalar_prefetch=1,
            grid=(blocks // per_step,),
            in_specs=[pl.BlockSpec(memory_space=pl.ANY)] * len(pieces)
            + [pl.BlockSpec((members, per_step * width // blocks), lambda i, s: (0, i))],
            out_specs=(
                pl.BlockSpec((per_step, kslots, members), lambda i, s: (i, 0, 0)),
                square,
                square,
            ),
            scratch_shapes=[
                pltpu.VMEM((len(pieces), edge, part), jnp.bfloat16),
                pltpu.VMEM(((4 * edge + 1) * lanes, 128), jnp.float32),
                pltpu.VMEM((per_step, kslots * lanes, 128), jnp.float32),
                pltpu.SemaphoreType.DMA((len(pieces),)),
            ],
        ),
        out_shape=(jax.ShapeDtypeStruct((blocks, kslots, members), jnp.bfloat16), squares, squares),
        compiler_params=pltpu.CompilerParams(vmem_limit_bytes=38 * 1024 * 1024),
        cost_estimate=pl.CostEstimate(
            flops=4 * blocks * kslots * kslots * members,
            bytes_accessed=16 * members * width,
            transcendentals=0,
        ),
        name="gather_gram",
    )(slots, *pieces, states)


def three_way(v):
    hi = v.astype(jnp.bfloat16)
    rest = v - hi.astype(jnp.float32)
    mid = rest.astype(jnp.bfloat16)
    low = (rest - mid.astype(jnp.float32)).astype(jnp.bfloat16)
    return hi, mid, low


def invert_kernel(gram_ref, out_ref, work):
    nblk, n, _ = gram_ref.shape
    lane = lax.broadcasted_iota(jnp.int32, (8, n), 1)
    sub = lax.broadcasted_iota(jnp.int32, (8, n), 0)
    lane2 = lax.broadcasted_iota(jnp.int32, (1, n), 1)
    rows = lax.broadcasted_iota(jnp.int32, (1, n, n), 1)
    cols = lax.broadcasted_iota(jnp.int32, (1, n, n), 2)
    work[...] = gram_ref[...] + jnp.where(rows == cols, 1.0, 0.0)

    for start in range(0, n, NB):
        panel = [[work[b, at : at + 8, :] for at in range(start, start + NB, 8)] for b in range(nblk)]
        for k in range(NB):
            here = lane == start + k
            own, at = divmod(k, 8)
            for b in range(nblk):
                col = [jnp.broadcast_to(p[:, start + k : start + k + 1], (8, n)) for p in panel[b]]
                inv = 1.0 / col[own][at : at + 1, :]
                scaled = jnp.where(here[0:1], inv, panel[b][own][at : at + 1, :] * inv)
                scaled = jnp.broadcast_to(scaled, (8, n))
                new = [jnp.where(here, 0.0, p) - c * scaled for p, c in zip(panel[b], col)]
                new[own] = jnp.where(sub == at, scaled, new[own])
                panel[b] = new
        inside = (lane2 >= start) & (lane2 < start + NB)
        for b in range(nblk):
            sides = work[b, start : start + NB, :]
            sides = jnp.where(lane2 < start, -sides, sides)
            done = jnp.concatenate(panel[b], axis=0)
            rh, rm, rl = three_way(done)
            ch, cm, cl = three_way(sides)
            rhs = jnp.concatenate([rh, rm, rh, rl, rm, rh, rl, rm], axis=0)
            lhs = jnp.concatenate([ch, ch, cm, ch, cm, cl, cm, cl], axis=0)
            change = dot(lhs, rhs, TN)
            for rows_at, count in ((0, start), (start + NB, n - NB - start)):
                if count:
                    rows = slice(rows_at, rows_at + count)
                    work[b, rows, :] = jnp.where(inside, 0.0, work[b, rows, :]) - change[rows]
            work[b, start : start + NB, :] = done

    out_ref[...] = work[...]


def invert(gram):
    return pl.pallas_call(
        invert_kernel,
        out_shape=jax.ShapeDtypeStruct(gram.shape, jnp.float32),
        scratch_shapes=[pltpu.VMEM(gram.shape, jnp.float32)],
        compiler_params=pltpu.CompilerParams(vmem_limit_bytes=10 * 1024 * 1024),
        name="invert_blocks",
    )(gram)


def update_kernel(inverse_ref, moved_ref, columns_ref, states_ref, out_ref):
    groups, rows, _ = out_ref.shape
    for at in range(inverse_ref.shape[0]):
        wh, wm, wl = three_way(inverse_ref[at])
        mh, mm, ml = three_way(moved_ref[at] * 0.5)
        solved = dot(
            jnp.concatenate([wh, wh, wm, wh, wl, wm], axis=1),
            jnp.concatenate([mh, mm, mh, ml, mh, mm], axis=0),
        )
        high = solved.astype(jnp.bfloat16)
        low = (solved - high.astype(jnp.float32)).astype(jnp.bfloat16)
        columns = columns_ref[at].T
        change = dot(
            jnp.concatenate([columns, columns], axis=1), jnp.concatenate([high, low], axis=0)
        )
        cells = slice(at * 128, at * 128 + 128)
        updated = (states_ref[:, cells].astype(jnp.float32) - change).astype(jnp.bfloat16)
        out_ref[:, :, cells] = updated.reshape(groups, rows, 128)


def update(inverse, moved, columns, states, groups, per_step=4):
    blocks, kslots, _ = inverse.shape
    square = pl.BlockSpec((per_step, kslots, kslots), lambda i: (i, 0, 0))
    members, width = states.shape
    return pl.pallas_call(
        update_kernel,
        grid=(blocks // per_step,),
        in_specs=[
            square,
            square,
            pl.BlockSpec((per_step, kslots, members), lambda i: (i, 0, 0)),
            pl.BlockSpec((members, per_step * kslots), lambda i: (0, i)),
        ],
        out_specs=pl.BlockSpec((groups, members // groups, per_step * kslots), lambda i: (0, 0, i)),
        out_shape=jax.ShapeDtypeStruct((groups, members // groups, width), jnp.bfloat16),
        compiler_params=pltpu.CompilerParams(vmem_limit_bytes=24 * 1024 * 1024),
        name="update",
    )(inverse, moved, columns, states)


def on_device(deviations, obs_cell, obs_weight, block_obs, block_count):
    groups = lax.axis_size("mem")
    members = deviations.shape[0] * groups
    obs_dev = obs_cell.shape[0]
    line_index = lax.axis_index("space") * groups + lax.axis_index("mem")
    local_index = block_obs - (line_index * obs_dev - obs_dev // 2)
    slot_ids = jnp.arange(block_obs.shape[1], dtype=jnp.int32)
    slots = jnp.where(slot_ids[None, :] < block_count[:, None], local_index, 2 * obs_dev)
    slots = slots.reshape(-1) * (members // 128)
    size = lax.axis_size("space") * groups
    up = [(i, i + 1) for i in range(size - 1)]
    down = [(b, a) for a, b in up]
    states = lax.all_to_all(deviations, "mem", split_axis=1, concat_axis=0, tiled=True)
    pieces = []
    for piece in range(PIECES):
        first, last = project(obs_cell, obs_weight, states, piece)
        low = lax.ppermute(last, ("space", "mem"), up)
        high = lax.ppermute(first, ("space", "mem"), down)
        pieces += [low, first, last, high]
    columns, gram, moved = gather_gram(slots, pieces, states, block_obs.shape[0])
    analysis = update(invert(gram), moved, columns, states, groups)
    return lax.all_to_all(
        analysis.reshape(members, -1), "mem", split_axis=0, concat_axis=1, tiled=True
    )


def solution(mesh):
    in_specs = (
        P("mem", "space"),
        P(("space", "mem")),
        P(("space", "mem")),
        P(("space", "mem"), None),
        P(("space", "mem")),
    )
    out_specs = P("mem", "space")

    return jax.shard_map(on_device, mesh=mesh, in_specs=in_specs, out_specs=out_specs, check_vma=False)
```
